32 devices in a mesh: grp: 2 (over y), var: 8 (over z, x), smp: 2 (over core).
Axes of the slice: x: 2, y: 2, z: 4, core: 2. Of those that a mesh axis runs over, the one named last changes fastest.
Arguments:
- genotypes: bfloat16 [15360, 1024], P(('grp', 'smp'), 'var'), parts along dimension 0, may hold values from 0 to 2, as said below
- ancestry_counts: int32 [15360, 32], P(('grp', 'smp')), parts along dimension 0, may hold values from 1 to 100
- residuals: int32 [15360, 16], P(('grp', 'smp')), parts along dimension 0, may hold values from -3000 to 3000
- freqs: float32 [64, 1024], P('grp', 'var'), parts along dimension 0, may hold values from 0.05 to 0.95
Outputs:
- q_new: float32 [15360, 32], P(('grp', 'smp', 'var')), parts along dimension 0
- q_gradient: float32 [15360, 32], P(('grp', 'smp', 'var')), parts along dimension 0
- p_new: float32 [64, 1024], P('grp', 'var'), parts along dimension 0
- p_gradient: float32 [64, 1024], P('grp', 'var'), parts along dimension 0
- z_score: float32 [64, 16, 1024], P('grp', None, 'var'), parts along dimension 0
The draws below stay inside these ranges and needn't reach their ends.
There are 2 independent parts, one for each index of `grp`. The reference program is written for one: setup_inputs(seed, part) draws one part's arguments, and reference() takes and returns one part's arrays. A program takes and returns all parts, laid end to end along the dimension named above; each array names one. Nothing has to cross between parts.
Inputs may be any that keep to these rules, and one draw needn't show every extreme that they name: `genotypes`: dosages lie in the closed range from 0 to 2.
All inputs are finite; a program needn't handle non-finite values.
Results may differ from the reference program's by a relative error of at most 0.0003.
Values sent between devices are 32-bit elements; how exact they have to be, the bound alone decides.
No kernel may reach another device: no remote copies, remote signals or barrier semaphores. Data moves between devices by JAX's collectives and lax.ppermute only.
A program may use at most 64 MiB of HBM per device.

```python
import math
import jax
import jax.numpy as jnp
from jax import lax

ANC = 32
TRAITS = 16
MV = 128
SAMPLES = 7680
VARIANTS = 1024
N_VAR = 8


def draw_genotypes(key, part):
    logits = jax.random.uniform(jax.random.fold_in(key, 11), (1, VARIANTS), jnp.float32, -2.5, 2.5)
    block_rows = 960
    block_ids = jnp.arange(SAMPLES // block_rows, dtype=jnp.int32)

    def one_block(block_index):
        block_key = jax.random.fold_in(jax.random.fold_in(key, 12), block_index)
        first_key, second_key = jax.random.split(block_key)
        noise_one = 2.0 * jax.random.normal(first_key, (block_rows, VARIANTS), jnp.float32)
        noise_two = 2.0 * jax.random.normal(second_key, (block_rows, VARIANTS), jnp.float32)
        dosage = jax.nn.sigmoid(logits + noise_one) + jax.nn.sigmoid(logits + noise_two)
        return dosage
    blocks = lax.map(one_block, block_ids)
    return blocks.reshape(SAMPLES, VARIANTS).astype(jnp.bfloat16)


def with_ends(array, key, low, largest):
    longest = array.shape.index(max(array.shape))
    spots = []
    for shift in (0, 1):
        where = [jax.random.randint(jax.random.fold_in(key, axis), (), 0, length) for axis, length in enumerate(array.shape)]
        where[longest] = (where[longest] + shift) % array.shape[longest]
        spots.append(tuple(where))
    return array.at[spots[0]].set(low).at[spots[1]].set(largest)


def levels(own_key, dims, pieces, least, top_value):
    gain = 1.0
    for axis_at, shards_of in pieces:
        steps = jax.random.uniform(jax.random.fold_in(jax.random.fold_in(own_key, 6), axis_at), (shards_of,), jnp.float32, least / len(pieces), top_value / len(pieces))
        gain = gain * jnp.repeat(jnp.exp(steps), dims[axis_at] // shards_of).reshape((-1,) + (1,) * (len(dims) - 1 - axis_at))
    return gain


def setup_inputs(seed: int = 0, part: int = 0) -> dict:
    splits = jax.random.split(jax.random.key(seed), 5)
    own_keys = jax.random.split(jax.random.fold_in(splits[4], part), 5)
    return {
        "genotypes": draw_genotypes(jax.random.fold_in(jax.random.fold_in(splits[4], part), 71), part),
        "ancestry_counts": with_ends(jax.random.randint(own_keys[1], (SAMPLES, ANC), 1, 101), jax.random.fold_in(own_keys[1], 1), 1, 100).astype(jnp.int32),
        "residuals": with_ends(jax.random.randint(own_keys[2], (SAMPLES, TRAITS), -3000, 3001), jax.random.fold_in(own_keys[2], 1), -3000, 3000).astype(jnp.int32),
        "freqs": jnp.clip(0.05 + 0.9 * jax.random.uniform(own_keys[3], (ANC, VARIANTS), jnp.float32) ** levels(own_keys[3], (ANC, VARIANTS), ((1, 8),), -0.2, 0.2), 0.05, 0.95),
    }


def reference(genotypes, ancestry_counts, residuals, freqs):
    highest = lax.Precision.HIGHEST
    counts = ancestry_counts.astype(jnp.float32)
    fractions = counts / lax.optimization_barrier(jnp.sum(counts, axis=1, keepdims=True))
    residual = residuals.astype(jnp.float32) / 1000.0
    column_ids = jnp.arange(N_VAR, dtype=jnp.int32)

    def first_pass(state_pair, column):
        gradient, second = state_pair
        start = (column * MV).astype(jnp.int32)
        dosage = lax.dynamic_slice_in_dim(genotypes, start, MV, 1).astype(jnp.float32)
        freq_block = lax.dynamic_slice_in_dim(freqs, start, MV, 1)
        recon_block = jnp.dot(fractions, freq_block, precision=highest)
        ratio_a = dosage / recon_block
        ratio_b = (2.0 - dosage) / (1.0 - recon_block)
        excess = ratio_a - ratio_b
        gradient = gradient + jnp.dot(excess, freq_block.T, precision=highest)
        second = second + lax.optimization_barrier(jnp.sum(ratio_b, axis=1))
        excess_block = jnp.dot(fractions.T, excess, precision=highest)
        second_block = jnp.dot(fractions.T, ratio_b, precision=highest)
        return ((gradient, second), (excess_block, second_block))
    start_pair = (jnp.zeros((SAMPLES, ANC), jnp.float32), jnp.zeros((SAMPLES,), jnp.float32))
    (gradient, second), (excess_blocks, second_blocks) = lax.scan(first_pass, start_pair, column_ids)
    excess_sum = excess_blocks.transpose(1, 0, 2).reshape(ANC, VARIANTS)
    second_sum = second_blocks.transpose(1, 0, 2).reshape(ANC, VARIANTS)
    q_gradient = gradient / math.sqrt(VARIANTS)
    weighted = fractions * (gradient + second[:, None])
    q_new = weighted / lax.optimization_barrier(jnp.sum(weighted, axis=1, keepdims=True))
    allele_sum = excess_sum + second_sum
    p_new = freqs * allele_sum / (freqs * allele_sum + (1.0 - freqs) * second_sum)
    p_gradient = excess_sum * ANC / math.sqrt(SAMPLES)
    trait_rows = (q_new[:, :, None] * residual[:, None, :]).reshape(SAMPLES, ANC * TRAITS)
    squares = q_new * q_new

    def second_pass(state_pair, column):
        start = (column * MV).astype(jnp.int32)
        dosage = lax.dynamic_slice_in_dim(genotypes, start, MV, 1).astype(jnp.float32)
        freq_block = lax.dynamic_slice_in_dim(freqs, start, MV, 1)
        ratio_next = dosage / jnp.dot(q_new, freq_block, precision=highest)
        score_block = jnp.dot(trait_rows.T, ratio_next, precision=highest)
        info_block = jnp.dot(squares.T, ratio_next * ratio_next, precision=highest)
        return (state_pair, (score_block, info_block))
    _, (score_blocks, info_blocks) = lax.scan(second_pass, jnp.zeros((), jnp.float32), column_ids)
    score = score_blocks.transpose(1, 0, 2).reshape(ANC, TRAITS, VARIANTS)
    information = info_blocks.transpose(1, 0, 2).reshape(ANC, VARIANTS)
    z_score = score / jnp.sqrt(information + 1e-06)[:, None, :]
    return (q_new, q_gradient, p_new, p_gradient, z_score)
```

```python
import functools
import math

import jax
import jax.numpy as jnp
from jax import lax
from jax.experimental import pallas as pl
from jax.experimental.pallas import tpu as pltpu
from jax.sharding import PartitionSpec as P

F32 = jnp.float32
BF16 = jnp.bfloat16


def split(x):
    high = x.astype(BF16)
    return high, (x - high.astype(F32)).astype(BF16)


def dot(a, b, dims):
    return lax.dot_general(a, b, (dims, ((), ())), preferred_element_type=F32)


NN = ((1,), (0,))
NT = ((1,), (1,))
TN = ((0,), (0,))


def first_kernel(geno_ref, counts_ref, freqs_ref, resid_ref, grad_ref, sums_ref, traits_ref):
    freqs = freqs_ref[...]
    freq_high, freq_low = split(freqs)
    ones = jnp.ones_like(freq_high)
    counts = counts_ref[...].astype(F32).astype(BF16)
    table = jnp.concatenate(
        [
            jnp.concatenate([freq_high, ones], axis=1),
            jnp.concatenate([freq_low, jnp.zeros_like(ones)], axis=1),
        ],
        axis=0,
    )
    width = freqs.shape[1]
    both = dot(jnp.concatenate([counts, counts], axis=1), table, NN)
    recon, total = both[:, :width], both[:, width:]
    rest = total - recon
    dosage = geno_ref[...].astype(F32)
    inverse = 1.0 / (recon * rest)
    part_b = (2.0 - dosage) * recon * inverse
    part = dosage * rest * inverse - part_b
    excess = part * total
    excess_high, excess_low = split(excess)
    left = jnp.concatenate([freq_high, freq_low], axis=0)
    left = jnp.concatenate([left, left], axis=1)
    right = jnp.concatenate([excess_high, excess_low], axis=1)
    grads = dot(left, right, NT)
    anc = freqs.shape[0]
    grad_ref[0] = grads[:anc] + grads[anc:]

    part_high, part_low = split(part)
    b_high, b_low = split(part_b)
    counts_t = counts.T
    sums = dot(counts_t, jnp.concatenate([part_high, b_high], axis=1), NN) + dot(
        counts_t, jnp.concatenate([part_low, b_low], axis=1), NN
    )

    @pl.when(pl.program_id(0) == 0)
    def _():
        sums_ref[...] = sums

    @pl.when(pl.program_id(0) > 0)
    def _():
        sums_ref[...] += sums

    traits_ref[0] = (resid_ref[...].astype(F32) / 1000.0).T


def share_kernel(variants, index_ref, parts_ref, counts_ref, q_ref, q_own_ref, g_own_ref):
    gradient = jnp.sum(parts_ref[...], axis=0)
    counts = counts_ref[...].astype(F32).T
    fractions = counts / jnp.sum(counts, axis=0, keepdims=True)
    second = 2.0 * variants - jnp.sum(fractions * gradient, axis=0, keepdims=True)
    weighted = fractions * (gradient + second)
    q_new = weighted / jnp.sum(weighted, axis=0, keepdims=True)
    for i in range(q_ref.shape[0]):
        q_ref[i] = q_new
    q_own_ref[...] = q_new.T
    g_own_ref[...] = (gradient / math.sqrt(variants)).T


def second_kernel(q_ref, geno_ref, traits_ref, freqs_ref, score_ref, info_ref):
    q_new = q_ref[0]
    anc, rows = q_new.shape
    freq_high, freq_low = split(freqs_ref[...])
    q_high, q_low = split(q_new)
    q_three = jnp.concatenate([q_high, q_low, q_high], axis=0)
    f_three = jnp.concatenate([freq_high, freq_high, freq_low], axis=0)
    recon = dot(q_three, f_three, TN)
    ratio = geno_ref[...].astype(F32) / recon
    ratio_high, ratio_low = split(ratio)
    traits = traits_ref[0]
    products = (q_new[:, None, :] * traits[None, :, :]).reshape(anc * traits.shape[0], rows)
    high, low = split(products)
    width = ratio.shape[1]
    wide = dot(high, jnp.concatenate([ratio_high, ratio_low], axis=1), NN)
    score = wide[:, :width] + wide[:, width:] + dot(low, ratio_high, NN)
    square_high, square_low = split(ratio * ratio)
    q2_high, q2_low = split(q_new * q_new)
    wide2 = dot(
        jnp.concatenate([q2_high, q2_low], axis=0),
        jnp.concatenate([square_high, square_low], axis=1),
        NN,
    )
    info = wide2[:anc, :width] + wide2[:anc, width:] + wide2[anc:, :width]

    @pl.when(pl.program_id(0) == 0)
    def _():
        score_ref[...] = score
        info_ref[...] = info

    @pl.when(pl.program_id(0) > 0)
    def _():
        score_ref[...] += score
        info_ref[...] += info


def update_freqs(freqs, excess_sum, second_sum, sample_count):
    allele_sum = excess_sum + second_sum
    freq_next = freqs * allele_sum / (freqs * allele_sum + (1.0 - freqs) * second_sum)
    freq_gradient = excess_sum * freqs.shape[0] / math.sqrt(sample_count)
    return (freq_next, freq_gradient)


def other_sum(tree):
    count = lax.axis_size("smp")
    if count != 2:
        return lax.psum(tree, "smp")
    swap = [(0, 1), (1, 0)]
    return jax.tree.map(lambda x: x + lax.ppermute(x, "smp", swap), tree)


def shards(genotypes, ancestry_counts, residuals, freqs):
    var_count = lax.axis_size("var")
    rows, width = genotypes.shape
    share = rows // var_count
    anc = freqs.shape[0]
    traits = residuals.shape[1]
    sample_count = rows * lax.axis_size("smp")
    variants = width * var_count
    shape = jax.ShapeDtypeStruct

    grads, sums, trait_cols = pl.pallas_call(
        first_kernel,
        grid=(var_count,),
        in_specs=[
            pl.BlockSpec((share, width), lambda i: (i, 0)),
            pl.BlockSpec((share, anc), lambda i: (i, 0)),
            pl.BlockSpec((anc, width), lambda i: (0, 0)),
            pl.BlockSpec((share, traits), lambda i: (i, 0)),
        ],
        out_specs=[
            pl.BlockSpec((1, anc, share), lambda i: (i, 0, 0)),
            pl.BlockSpec((anc, 2 * width), lambda i: (0, 0)),
            pl.BlockSpec((1, traits, share), lambda i: (i, 0, 0)),
        ],
        out_shape=[
            shape((var_count, anc, share), F32),
            shape((anc, 2 * width), F32),
            shape((var_count, traits, share), F32),
        ],
        name="first",
    )(genotypes, ancestry_counts, freqs, residuals)

    parts = lax.all_to_all(grads, "var", 0, 0, tiled=True)

    sums_all = other_sum(sums)
    freq_next, freq_gradient = update_freqs(
        freqs, sums_all[:, :width], sums_all[:, width:], sample_count
    )

    own = lax.axis_index("var").astype(jnp.int32).reshape(1)
    q_send, own_next, own_gradient = pl.pallas_call(
        functools.partial(share_kernel, variants),
        grid_spec=pltpu.PrefetchScalarGridSpec(
            num_scalar_prefetch=1,
            grid=(1,),
            in_specs=[
                pl.BlockSpec((var_count, anc, share), lambda i, own: (0, 0, 0)),
                pl.BlockSpec((share, anc), lambda i, own: (own[0], 0)),
            ],
            out_specs=[
                pl.BlockSpec((var_count, anc, share), lambda i, own: (0, 0, 0)),
                pl.BlockSpec((share, anc), lambda i, own: (0, 0)),
                pl.BlockSpec((share, anc), lambda i, own: (0, 0)),
            ],
        ),
        out_shape=[
            shape((var_count, anc, share), F32),
            shape((share, anc), F32),
            shape((share, anc), F32),
        ],
        name="share",
    )(own, parts, ancestry_counts)

    q_all = lax.all_to_all(q_send, "var", 0, 0, tiled=True)

    score, info = pl.pallas_call(
        second_kernel,
        grid=(var_count,),
        in_specs=[
            pl.BlockSpec((1, anc, share), lambda i: (i, 0, 0)),
            pl.BlockSpec((share, width), lambda i: (i, 0)),
            pl.BlockSpec((1, traits, share), lambda i: (i, 0, 0)),
            pl.BlockSpec((anc, width), lambda i: (0, 0)),
        ],
        out_specs=[
            pl.BlockSpec((anc * traits, width), lambda i: (0, 0)),
            pl.BlockSpec((anc, width), lambda i: (0, 0)),
        ],
        out_shape=[shape((anc * traits, width), F32), shape((anc, width), F32)],
        name="second",
    )(q_all, genotypes, trait_cols, freqs)

    score, info = other_sum((score, info))
    tiles = score.reshape(anc, traits, width)
    z_score = tiles / jnp.sqrt(info + 1e-06)[:, None, :]
    return (own_next, own_gradient, freq_next, freq_gradient, z_score)


def plain_shards(genotypes, ancestry_counts, residuals, freqs):
    highest = lax.Precision.HIGHEST
    var_count = lax.axis_size("var")
    rows, width = genotypes.shape
    share = rows // var_count
    anc = freqs.shape[0]
    traits = residuals.shape[1]
    counts = ancestry_counts.astype(F32)
    fractions = counts / jnp.sum(counts, axis=1, keepdims=True)
    dosage = genotypes.astype(F32)
    recon = jnp.dot(fractions, freqs, precision=highest)
    ratio_a = dosage / recon
    ratio_b = (2.0 - dosage) / (1.0 - recon)
    excess = ratio_a - ratio_b
    gradient, second = lax.psum(
        (jnp.dot(excess, freqs.T, precision=highest), jnp.sum(ratio_b, axis=1)), "var"
    )
    excess_sum, second_sum = lax.psum(
        (
            jnp.dot(fractions.T, excess, precision=highest),
            jnp.dot(fractions.T, ratio_b, precision=highest),
        ),
        "smp",
    )
    freq_next, freq_gradient = update_freqs(
        freqs, excess_sum, second_sum, rows * lax.axis_size("smp")
    )
    weighted = fractions * (gradient + second[:, None])
    q_new = weighted / jnp.sum(weighted, axis=1, keepdims=True)
    first_row = lax.axis_index("var") * share
    own_next = lax.dynamic_slice_in_dim(q_new, first_row, share, 0)
    own_gradient = lax.dynamic_slice_in_dim(gradient, first_row, share, 0)
    ratio = dosage / jnp.dot(q_new, freqs, precision=highest)
    residual = residuals.astype(F32) / 1000.0
    products = (q_new[:, :, None] * residual[:, None, :]).reshape(rows, anc * traits)
    score, info = lax.psum(
        (
            jnp.dot(products.T, ratio, precision=highest),
            jnp.dot((q_new * q_new).T, ratio * ratio, precision=highest),
        ),
        "smp",
    )
    tiles = score.reshape(anc, traits, width)
    z_score = tiles / jnp.sqrt(info + 1e-06)[:, None, :]
    return (own_next, own_gradient / math.sqrt(width * var_count), freq_next, freq_gradient, z_score)


def solution(mesh):
    sizes = dict(mesh.shape)

    def step(genotypes, ancestry_counts, residuals, freqs):
        rows = genotypes.shape[0] // (sizes["grp"] * sizes["smp"])
        whole_tiles = rows % (16 * sizes["var"]) == 0
        in_specs = (
            P(("grp", "smp"), "var"),
            P(("grp", "smp"), None),
            P(("grp", "smp"), None),
            P("grp", "var"),
        )
        out_specs = (
            P(("grp", "smp", "var"), None),
            P(("grp", "smp", "var"), None),
            P("grp", "var"),
            P("grp", "var"),
            P("grp", None, "var"),
        )
        return jax.shard_map(
            shards if whole_tiles else plain_shards,
            mesh=mesh,
            in_specs=in_specs,
            out_specs=out_specs,
            check_vma=False,
        )(genotypes, ancestry_counts, residuals, freqs)

    return step
```

```python
import functools
import math

import jax
import jax.numpy as jnp
from jax import lax
from jax.experimental import pallas as pl
from jax.experimental.pallas import tpu as pltpu
from jax.sharding import PartitionSpec as P

F32 = jnp.float32
BF16 = jnp.bfloat16
LANES = 128
NN = ((1,), (0,))
NT = ((1,), (1,))
TN = ((0,), (0,))


def split(x):
    high = x.astype(BF16)
    return high, (x - high.astype(F32)).astype(BF16)


def dot(a, b, dims):
    return lax.dot_general(a, b, (dims, ((), ())), preferred_element_type=F32)


def count_table(freqs):
    high, low = split(freqs)
    ones = jnp.ones_like(high)
    return jnp.concatenate(
        [
            jnp.concatenate([high, ones], axis=1),
            jnp.concatenate([low, jnp.zeros_like(ones)], axis=1),
        ],
        axis=0,
    )


def ratio_parts(counts, dosage, table):
    width = dosage.shape[1]
    both = dot(jnp.concatenate([counts, counts], axis=0), table, TN)
    recon, total = both[:, :width], both[:, width:]
    rest = total - recon
    inverse = 1.0 / (recon * rest)
    part_b = (2.0 - dosage) * recon * inverse
    part = dosage * rest * inverse - part_b
    return part, part_b, total


def gradient_kernel(shares, place_ref, geno_ref, counts_ref, freqs_ref, grad_ref, excess_ref):
    half_rows = excess_ref.shape[0]
    width = freqs_ref.shape[1]
    anc = freqs_ref.shape[0]
    start = place_ref[0] * half_rows
    freqs = freqs_ref[...]
    table = count_table(freqs)
    for row in range(0, half_rows, LANES):
        first = pl.multiple_of(start + row, LANES)
        counts = counts_ref[:, pl.ds(first, LANES)].astype(F32).astype(BF16)
        dosage = geno_ref[pl.ds(first, LANES), :].astype(F32)
        part, _, total = ratio_parts(counts, dosage, table)
        high, low = split(part * total)
        excess_ref[pl.ds(row, LANES), :width] = high
        excess_ref[pl.ds(row, LANES), width:] = low
    left = jnp.concatenate(split(freqs), axis=0)
    grads = dot(jnp.concatenate([left, left], axis=1), excess_ref[...], NT)
    grads = grads[:anc] + grads[anc:]
    share = half_rows // shares
    for c in range(shares):
        grad_ref[c ^ place_ref[1]] = grads[:, c * share : (c + 1) * share]


def sums_kernel(geno_ref, counts_ref, freqs_ref, resid_ref, sums_ref, traits_ref, own_ref, parts_ref):
    rows, width = geno_ref.shape
    table = count_table(freqs_ref[...])
    for row in range(0, rows, LANES):
        counts = counts_ref[:, pl.ds(row, LANES)].astype(F32).astype(BF16)
        dosage = geno_ref[pl.ds(row, LANES), :].astype(F32)
        part, part_b, _ = ratio_parts(counts, dosage, table)
        for at, value in enumerate((part, part_b)):
            high, low = split(value)
            parts_ref[pl.ds(row, LANES), pl.ds(at * width, width)] = high
            parts_ref[pl.ds(rows + row, LANES), pl.ds(at * width, width)] = low
    counts = counts_ref[...].astype(F32)
    left = counts.astype(BF16)
    sums_ref[...] = dot(jnp.concatenate([left, left], axis=1), parts_ref[...], NN)
    residual = resid_ref[...].astype(F32) / 1000.0
    share = traits_ref.shape[2]
    for c in range(rows // share):
        traits_ref[c] = residual[:, c * share : (c + 1) * share]
        own_ref[c] = counts[:, c * share : (c + 1) * share]


def share_kernel(variants, n_parts, own_ref, counts_ref, *refs):
    parts, (q_ref, grad_ref) = refs[:n_parts], refs[n_parts:]
    gradient = parts[0][...]
    for part in parts[1:]:
        gradient = gradient + part[...]
    counts = counts_ref[own_ref[0]]
    fractions = counts / jnp.sum(counts, axis=0, keepdims=True)
    second = 2.0 * variants - jnp.sum(fractions * gradient, axis=0, keepdims=True)
    weighted = fractions * (gradient + second)
    q_ref[...] = weighted / jnp.sum(weighted, axis=0, keepdims=True)
    grad_ref[...] = gradient / math.sqrt(variants)


def score_kernel(n_shares, fresh, own_ref, *refs):
    q_refs, refs = refs[:n_shares], refs[n_shares:]
    geno_ref, traits_ref, freqs_ref = refs[:3]
    total_ref = None if fresh else refs[3]
    out_ref = refs[-1]
    freq_high, freq_low = split(freqs_ref[...])
    f_three = jnp.concatenate([freq_high, freq_high, freq_low], axis=0)
    anc, width = freqs_ref.shape
    traits = traits_ref.shape[1]
    score, info = None, None
    for c in range(n_shares):
        q_new = q_refs[c][...]
        rows = q_new.shape[1]
        owner = own_ref[c]
        q_high, q_low = split(q_new)
        recon = dot(jnp.concatenate([q_high, q_low, q_high], axis=0), f_three, TN)
        dosage = geno_ref[pl.ds(pl.multiple_of(owner * rows, 16), rows), :].astype(F32)
        ratio = dosage / recon
        ratio_high, ratio_low = split(ratio)
        right = jnp.concatenate([ratio_high, ratio_low], axis=1)
        square_high, square_low = split(ratio * ratio)
        q2_high, q2_low = split(q_new * q_new)
        residual = traits_ref[owner]
        products = (q_new[:, None, :] * residual[None, :, :]).reshape(anc * traits, rows)
        high, low = split(products)
        wide = dot(high, right, NN)
        part = wide[:, :width] + wide[:, width:] + dot(low, ratio_high, NN)
        wide2 = dot(
            jnp.concatenate([q2_high, q2_low], axis=0),
            jnp.concatenate([square_high, square_low], axis=1),
            NN,
        )
        part2 = wide2[:anc, :width] + wide2[:anc, width:] + wide2[anc:, :width]
        score = part if score is None else score + part
        info = part2 if info is None else info + part2
    if not fresh:
        score = score + total_ref[: anc * traits]
        info = info + total_ref[anc * traits :]
    out_ref[: anc * traits] = score
    out_ref[anc * traits :] = info


def final_kernel(mine_ref, other_ref, out_ref):
    anc, traits, width = out_ref.shape
    total = mine_ref[...] + other_ref[...]
    scale = jnp.sqrt(total[anc * traits :] + 1e-06)
    out_ref[...] = total[: anc * traits].reshape(anc, traits, width) / scale[:, None, :]


def update_freqs(freqs, excess_sum, second_sum, sample_count):
    allele_sum = excess_sum + second_sum
    freq_next = freqs * allele_sum / (freqs * allele_sum + (1.0 - freqs) * second_sum)
    freq_gradient = excess_sum * freqs.shape[0] / math.sqrt(sample_count)
    return (freq_next, freq_gradient)


VMEM = pltpu.VMEM
SCALARS = pl.BlockSpec(memory_space=pltpu.SMEM)
IN_VMEM = pl.BlockSpec(memory_space=pltpu.VMEM)


def call(kernel, name, n_scalars, args, outs, scratch=(), cost=2000, aliases=None):
    args = args[:n_scalars] + tuple(pltpu.with_memory_space_constraint(x, VMEM) for x in args[n_scalars:])
    return pl.pallas_call(
        kernel,
        in_specs=[SCALARS] * n_scalars + [IN_VMEM] * (len(args) - n_scalars),
        out_specs=[IN_VMEM] * len(outs),
        out_shape=[VMEM(s, F32) for s in outs],
        scratch_shapes=list(scratch),
        input_output_aliases=aliases or {},
        cost_estimate=pl.CostEstimate(flops=cost * 400_000, bytes_accessed=0, transcendentals=0),
        name=name,
    )(*args)


def shards(genotypes, ancestry_counts, residuals, freqs):
    var_count = lax.axis_size("var")
    rows, width = genotypes.shape
    share = rows // var_count
    half = var_count // 2
    anc = freqs.shape[0]
    traits = residuals.shape[1]
    sample_count = rows * lax.axis_size("smp")
    variants = width * var_count
    place = lax.axis_index("var").astype(jnp.int32)

    def move(x, m):
        return lax.ppermute(x, "var", [(i, i ^ m) for i in range(var_count)])

    def swap(x):
        return lax.ppermute(x, "smp", [(0, 1), (1, 0)])

    geno = pltpu.with_memory_space_constraint(genotypes, VMEM)
    counts = pltpu.with_memory_space_constraint(ancestry_counts.T, VMEM)
    resid = residuals.T

    def gradients(which, name):
        scalars = jnp.stack([which, place % half])
        (grads,) = call(
            functools.partial(gradient_kernel, half),
            name,
            1,
            (scalars, geno, counts, freqs),
            [(half, anc, share)],
            [VMEM((rows // 2, 2 * width), BF16)],
        )
        return grads

    far = gradients(1 - place // half, "grad_far")
    far_even = far.reshape(half // 2, 2, anc, share)
    got = move(far_even[:, 1], 1)
    near = gradients(place // half, "grad_near")
    arrived = [near[0]] + [move(near[m], m) for m in range(1, half)]
    combined = far_even[:, 0] + got
    arrived += [move(combined[m], half + 2 * m) for m in range(half // 2)]

    sums, trait_parts, count_parts = call(
        sums_kernel,
        "sums",
        0,
        (geno, counts, freqs, resid),
        [(anc, 2 * width), (var_count, traits, share), (var_count, anc, share)],
        [VMEM((2 * rows, 2 * width), BF16)],
    )
    sums_all = sums + swap(sums)
    freq_next, freq_gradient = update_freqs(
        freqs, sums_all[:, :width], sums_all[:, width:], sample_count
    )

    own = place.reshape(1)
    q_new, own_gradient = call(
        functools.partial(share_kernel, variants, len(arrived)),
        "share",
        1,
        (own, count_parts, *arrived),
        [(anc, share), (anc, share)],
        cost=500,
    )

    shares = {m: move(q_new, m) for m in range(2, var_count, 2)}
    shares[1] = move(q_new, 1)
    for m in range(3, half, 2):
        shares[m] = move(q_new, m)
    for m in range(half + 1, var_count, 2):
        shares[m] = move(shares[m - 1], 1)
    shares[0] = q_new

    def scores(ms, total):
        owners = jnp.stack([place ^ m for m in ms])
        inputs = (geno, trait_parts, freqs) + (() if total is None else (total,))
        (out,) = call(
            functools.partial(score_kernel, len(ms), total is None),
            "score",
            1,
            (owners, *[shares[m] for m in ms], *inputs),
            [((anc * traits + anc), width)],
            cost=700 * len(ms),
            aliases=None if total is None else {len(ms) + 4: 0},
        )
        return out

    order = [0, 1] + list(range(2, half)) + list(range(half, var_count, 2)) + list(range(half + 1, var_count, 2))
    total = None
    for at in range(0, var_count, 2):
        total = scores(order[at : at + 2], total)
    (z_score,) = call(final_kernel, "final", 0, (total, swap(total)), [(anc, traits, width)], cost=300)
    return (q_new.T, own_gradient.T, freq_next, freq_gradient, z_score)


def plain_shards(genotypes, ancestry_counts, residuals, freqs):
    highest = lax.Precision.HIGHEST
    var_count = lax.axis_size("var")
    rows, width = genotypes.shape
    share = rows // var_count
    anc = freqs.shape[0]
    traits = residuals.shape[1]
    counts = ancestry_counts.astype(F32)
    fractions = counts / jnp.sum(counts, axis=1, keepdims=True)
    dosage = genotypes.astype(F32)
    recon = jnp.dot(fractions, freqs, precision=highest)
    ratio_a = dosage / recon
    ratio_b = (2.0 - dosage) / (1.0 - recon)
    excess = ratio_a - ratio_b
    gradient, second = lax.psum(
        (jnp.dot(excess, freqs.T, precision=highest), jnp.sum(ratio_b, axis=1)), "var"
    )
    excess_sum, second_sum = lax.psum(
        (
            jnp.dot(fractions.T, excess, precision=highest),
            jnp.dot(fractions.T, ratio_b, precision=highest),
        ),
        "smp",
    )
    freq_next, freq_gradient = update_freqs(
        freqs, excess_sum, second_sum, rows * lax.axis_size("smp")
    )
    weighted = fractions * (gradient + second[:, None])
    q_new = weighted / jnp.sum(weighted, axis=1, keepdims=True)
    first_row = lax.axis_index("var") * share
    own_next = lax.dynamic_slice_in_dim(q_new, first_row, share, 0)
    own_gradient = lax.dynamic_slice_in_dim(gradient, first_row, share, 0)
    ratio = dosage / jnp.dot(q_new, freqs, precision=highest)
    residual = residuals.astype(F32) / 1000.0
    products = (q_new[:, :, None] * residual[:, None, :]).reshape(rows, anc * traits)
    score, info = lax.psum(
        (
            jnp.dot(products.T, ratio, precision=highest),
            jnp.dot((q_new * q_new).T, ratio * ratio, precision=highest),
        ),
        "smp",
    )
    tiles = score.reshape(anc, traits, width)
    z_score = tiles / jnp.sqrt(info + 1e-06)[:, None, :]
    return (own_next, own_gradient / math.sqrt(width * var_count), freq_next, freq_gradient, z_score)


def solution(mesh):
    sizes = dict(mesh.shape)

    def step(genotypes, ancestry_counts, residuals, freqs):
        rows = genotypes.shape[0] // (sizes["grp"] * sizes["smp"])
        power = sizes["var"] & (sizes["var"] - 1) == 0 and sizes["var"] >= 4
        tiled = rows % (16 * sizes["var"]) == 0 and rows % (2 * LANES) == 0
        in_specs = (
            P(("grp", "smp"), "var"),
            P(("grp", "smp"), None),
            P(("grp", "smp"), None),
            P("grp", "var"),
        )
        out_specs = (
            P(("grp", "smp", "var"), None),
            P(("grp", "smp", "var"), None),
            P("grp", "var"),
            P("grp", "var"),
            P("grp", None, "var"),
        )
        return jax.shard_map(
            shards if power and tiled and sizes["smp"] == 2 else plain_shards,
            mesh=mesh,
            in_specs=in_specs,
            out_specs=out_specs,
            check_vma=False,
        )(genotypes, ancestry_counts, residuals, freqs)

    return step
```

```python
import functools
import math

import jax
import jax.numpy as jnp
from jax import lax
from jax.experimental import pallas as pl
from jax.experimental.pallas import tpu as pltpu
from jax.sharding import PartitionSpec as P

F32 = jnp.float32
BF16 = jnp.bfloat16
LANES = 128
NN = ((1,), (0,))
NT = ((1,), (1,))
TN = ((0,), (0,))


def split(x):
    high = x.astype(BF16)
    return high, (x - high.astype(F32)).astype(BF16)


def dot(a, b, dims):
    return lax.dot_general(a, b, (dims, ((), ())), preferred_element_type=F32)


def count_table(freqs):
    high, low = split(freqs)
    ones = jnp.ones_like(high)
    return jnp.concatenate(
        [
            jnp.concatenate([high, ones], axis=1),
            jnp.concatenate([low, jnp.zeros_like(ones)], axis=1),
        ],
        axis=0,
    )


def ratio_parts(counts, dosage, table):
    width = dosage.shape[1]
    both = dot(jnp.concatenate([counts, counts], axis=0), table, TN)
    recon, total = both[:, :width], both[:, width:]
    rest = total - recon
    inverse = 1.0 / (recon * rest)
    part_b = (2.0 - dosage) * recon * inverse
    part = dosage * rest * inverse - part_b
    return part, part_b, total


def gradient_kernel(shares, far, place_ref, geno_ref, counts_ref, freqs_ref, grad_ref, excess_ref, *copies):
    half_rows = excess_ref.shape[0]
    width = freqs_ref.shape[1]
    anc = freqs_ref.shape[0]
    own_half = place_ref[0] // shares
    start = (1 - own_half if far else own_half) * half_rows
    if far:
        geno_buf, counts_buf, sems = copies
        pieces = sems.shape[1]
        size = half_rows // pieces
        moves = []
        for i in range(pieces):
            first = pl.multiple_of(start + i * size, LANES)
            rows = pl.ds(i * size, size)
            moves.append(
                (
                    pltpu.make_async_copy(
                        counts_ref.at[:, pl.ds(first, size)], counts_buf.at[:, rows], sems.at[0, i]
                    ),
                    pltpu.make_async_copy(
                        geno_ref.at[pl.ds(first, size), :], geno_buf.at[rows, :], sems.at[1, i]
                    ),
                )
            )
            for copy in moves[-1]:
                copy.start()
    freqs = freqs_ref[...]
    table = count_table(freqs)
    for row in range(0, half_rows, LANES):
        if far:
            if row % size == 0:
                for copy in moves[row // size]:
                    copy.wait()
            counts = counts_buf[:, pl.ds(row, LANES)]
            dosage = geno_buf[pl.ds(row, LANES), :]
        else:
            first = pl.multiple_of(start + row, LANES)
            counts = counts_ref[:, pl.ds(first, LANES)]
            dosage = geno_ref[pl.ds(first, LANES), :]
        part, _, total = ratio_parts(counts.astype(F32).astype(BF16), dosage.astype(F32), table)
        high, low = split(part * total)
        excess_ref[pl.ds(row, LANES), :width] = high
        excess_ref[pl.ds(row, LANES), width:] = low
    left = jnp.concatenate(split(freqs), axis=0)
    grads = dot(jnp.concatenate([left, left], axis=1), excess_ref[...], NT)
    grads = grads[:anc] + grads[anc:]
    share = half_rows // shares
    for c in range(shares):
        grad_ref[c ^ (place_ref[0] % shares)] = grads[:, c * share : (c + 1) * share]


def sums_kernel(place_ref, geno_ref, counts_ref, freqs_ref, resid_ref, sums_ref, traits_ref, own_ref, parts_ref):
    rows, width = geno_ref.shape
    table = count_table(freqs_ref[...])
    for row in range(0, rows, LANES):
        counts = counts_ref[:, pl.ds(row, LANES)].astype(F32).astype(BF16)
        dosage = geno_ref[pl.ds(row, LANES), :].astype(F32)
        part, part_b, _ = ratio_parts(counts, dosage, table)
        for at, value in enumerate((part, part_b)):
            high, low = split(value)
            parts_ref[pl.ds(row, LANES), pl.ds(at * width, width)] = high
            parts_ref[pl.ds(rows + row, LANES), pl.ds(at * width, width)] = low
    counts = counts_ref[...].astype(F32)
    left = counts.astype(BF16)
    sums_ref[...] = dot(jnp.concatenate([left, left], axis=1), parts_ref[...], NN)
    residual = resid_ref[...].astype(F32) / 1000.0
    share = traits_ref.shape[2]
    for c in range(rows // share):
        traits_ref[c] = residual[:, c * share : (c + 1) * share]
        own_ref[c] = counts[:, c * share : (c + 1) * share]


def share_kernel(variants, own_ref, counts_ref, total_ref, q_ref, grad_ref):
    gradient = total_ref[...]
    counts = counts_ref[own_ref[0]]
    fractions = counts / jnp.sum(counts, axis=0, keepdims=True)
    second = 2.0 * variants - jnp.sum(fractions * gradient, axis=0, keepdims=True)
    weighted = fractions * (gradient + second)
    q_ref[...] = weighted / jnp.sum(weighted, axis=0, keepdims=True)
    grad_ref[...] = gradient / math.sqrt(variants)


def score_kernel(shares, fresh, own_ref, *refs):
    q_refs, refs = refs[: len(shares)], refs[len(shares) :]
    geno_ref, traits_ref, freqs_ref = refs[:3]
    total_ref = None if fresh else refs[3]
    out_ref = refs[-1]
    freq_high, freq_low = split(freqs_ref[...])
    f_three = jnp.concatenate([freq_high, freq_high, freq_low], axis=0)
    anc, width = freqs_ref.shape
    traits = traits_ref.shape[1]
    score, info = None, None
    for m, q_ref in zip(shares, q_refs):
        q_new = q_ref[...]
        rows = q_new.shape[1]
        owner = own_ref[0] ^ m
        q_high, q_low = split(q_new)
        recon = dot(jnp.concatenate([q_high, q_low, q_high], axis=0), f_three, TN)
        dosage = geno_ref[pl.ds(pl.multiple_of(owner * rows, 16), rows), :].astype(F32)
        ratio = dosage / recon
        ratio_high, ratio_low = split(ratio)
        right = jnp.concatenate([ratio_high, ratio_low], axis=1)
        square_high, square_low = split(ratio * ratio)
        q2_high, q2_low = split(q_new * q_new)
        residual = traits_ref[owner]
        products = (q_new[:, None, :] * residual[None, :, :]).reshape(anc * traits, rows)
        high, low = split(products)
        wide = dot(high, right, NN)
        part = wide[:, :width] + wide[:, width:] + dot(low, ratio_high, NN)
        wide2 = dot(
            jnp.concatenate([q2_high, q2_low], axis=0),
            jnp.concatenate([square_high, square_low], axis=1),
            NN,
        )
        part2 = wide2[:anc, :width] + wide2[:anc, width:] + wide2[anc:, :width]
        score = part if score is None else score + part
        info = part2 if info is None else info + part2
    if not fresh:
        score = score + total_ref[: anc * traits]
        info = info + total_ref[anc * traits :]
    out_ref[: anc * traits] = score
    out_ref[anc * traits :] = info


def final_kernel(place_ref, mine_ref, other_ref, out_ref):
    anc, traits, width = out_ref.shape
    total = mine_ref[...] + other_ref[...]
    scale = jnp.sqrt(total[anc * traits :] + 1e-06)
    out_ref[...] = total[: anc * traits].reshape(anc, traits, width) / scale[:, None, :]


def update_freqs(freqs, excess_sum, second_sum, sample_count):
    allele_sum = excess_sum + second_sum
    freq_next = freqs * allele_sum / (freqs * allele_sum + (1.0 - freqs) * second_sum)
    freq_gradient = excess_sum * freqs.shape[0] / math.sqrt(sample_count)
    return (freq_next, freq_gradient)


VMEM = pltpu.VMEM
SCALARS = pl.BlockSpec(memory_space=pltpu.SMEM)
IN_VMEM = pl.BlockSpec(memory_space=pltpu.VMEM)


def call(kernel, name, args, outs, scratch=(), cost=2000, aliases=None, raw=()):
    specs = [SCALARS]
    held = [args[0]]
    for at, x in enumerate(args[1:], 1):
        specs.append(pl.BlockSpec(memory_space=pl.ANY) if at in raw else IN_VMEM)
        held.append(x if at in raw else pltpu.with_memory_space_constraint(x, VMEM))
    return pl.pallas_call(
        kernel,
        in_specs=specs,
        out_specs=[IN_VMEM] * len(outs),
        out_shape=[VMEM(s, F32) for s in outs],
        scratch_shapes=list(scratch),
        input_output_aliases=aliases or {},
        cost_estimate=pl.CostEstimate(flops=cost * 400_000, bytes_accessed=0, transcendentals=0),
        name=name,
    )(*held)


def shards(genotypes, ancestry_counts, residuals, freqs):
    var_count = lax.axis_size("var")
    rows, width = genotypes.shape
    share = rows // var_count
    half = var_count // 2
    anc = freqs.shape[0]
    traits = residuals.shape[1]
    sample_count = rows * lax.axis_size("smp")
    variants = width * var_count
    place = lax.axis_index("var").astype(jnp.int32).reshape(1)

    def move(x, m, name):
        with jax.named_scope(name):
            return lax.ppermute(x, "var", [(i, i ^ m) for i in range(var_count)])

    def swap(x, name):
        with jax.named_scope(name):
            return lax.ppermute(x, "smp", [(0, 1), (1, 0)])

    counts = ancestry_counts.T
    resid = residuals.T
    half_rows = rows // 2
    excess = VMEM((half_rows, 2 * width), BF16)
    pieces = 3 if half_rows % (3 * LANES) == 0 else 1

    (far,) = call(
        functools.partial(gradient_kernel, half, True),
        "grad_far",
        (place, genotypes, counts, freqs),
        [(half, anc, share)],
        [
            excess,
            VMEM((half_rows, width), BF16),
            VMEM((anc, half_rows), jnp.int32),
            pltpu.SemaphoreType.DMA((2, pieces)),
        ],
        raw=(1, 2),
    )
    (near,) = call(
        functools.partial(gradient_kernel, half, False),
        "grad_near",
        (place, genotypes, counts, freqs),
        [(half, anc, share)],
        [excess],
    )
    slots = {half + c: far[c] for c in range(half)} | {c: near[c] for c in range(half)}
    bit = 1
    while bit < var_count:
        for m in reversed(range(bit, var_count, 2 * bit)):
            slots[m ^ bit] = slots[m ^ bit] + move(slots[m], bit, f"rs{m}")
        bit *= 2

    sums, trait_parts, count_parts = call(
        sums_kernel,
        "sums",
        (place, genotypes, counts, freqs, resid),
        [(anc, 2 * width), (var_count, traits, share), (var_count, anc, share)],
        [VMEM((2 * rows, 2 * width), BF16)],
    )
    sums_all = sums + swap(sums, "swap_sums")
    freq_next, freq_gradient = update_freqs(
        freqs, sums_all[:, :width], sums_all[:, width:], sample_count
    )

    q_new, own_gradient = call(
        functools.partial(share_kernel, variants),
        "share",
        (place, count_parts, slots[0]),
        [(anc, share), (anc, share)],
        cost=500,
    )

    shares = {0: q_new}
    bit = half
    while bit:
        for m in range(bit, var_count, 2 * bit):
            shares[m] = move(shares[m ^ bit], bit, f"ag{m}")
        bit //= 2

    def scores(ms, total):
        inputs = (genotypes, trait_parts, freqs) + (() if total is None else (total,))
        (out,) = call(
            functools.partial(score_kernel, ms, total is None),
            "score",
            (place, *[shares[m] for m in ms], *inputs),
            [((anc * traits + anc), width)],
            cost=700 * len(ms),
            aliases=None if total is None else {len(ms) + 4: 0},
        )
        return out

    total = None
    for ms in ([0], [2], [1], [3], [4], [6], [5], [7]) if var_count == 8 else [[m] for m in range(var_count)]:
        total = scores(tuple(ms), total)
    (z_score,) = call(
        final_kernel, "final", (place, total, swap(total, "swap_score")), [(anc, traits, width)], cost=300
    )
    return (q_new.T, own_gradient.T, freq_next, freq_gradient, z_score)


def plain_shards(genotypes, ancestry_counts, residuals, freqs):
    highest = lax.Precision.HIGHEST
    var_count = lax.axis_size("var")
    rows, width = genotypes.shape
    share = rows // var_count
    anc = freqs.shape[0]
    traits = residuals.shape[1]
    counts = ancestry_counts.astype(F32)
    fractions = counts / jnp.sum(counts, axis=1, keepdims=True)
    dosage = genotypes.astype(F32)
    recon = jnp.dot(fractions, freqs, precision=highest)
    ratio_a = dosage / recon
    ratio_b = (2.0 - dosage) / (1.0 - recon)
    excess = ratio_a - ratio_b
    gradient, second = lax.psum(
        (jnp.dot(excess, freqs.T, precision=highest), jnp.sum(ratio_b, axis=1)), "var"
    )
    excess_sum, second_sum = lax.psum(
        (
            jnp.dot(fractions.T, excess, precision=highest),
            jnp.dot(fractions.T, ratio_b, precision=highest),
        ),
        "smp",
    )
    freq_next, freq_gradient = update_freqs(
        freqs, excess_sum, second_sum, rows * lax.axis_size("smp")
    )
    weighted = fractions * (gradient + second[:, None])
    q_new = weighted / jnp.sum(weighted, axis=1, keepdims=True)
    first_row = lax.axis_index("var") * share
    own_next = lax.dynamic_slice_in_dim(q_new, first_row, share, 0)
    own_gradient = lax.dynamic_slice_in_dim(gradient, first_row, share, 0)
    ratio = dosage / jnp.dot(q_new, freqs, precision=highest)
    residual = residuals.astype(F32) / 1000.0
    products = (q_new[:, :, None] * residual[:, None, :]).reshape(rows, anc * traits)
    score, info = lax.psum(
        (
            jnp.dot(products.T, ratio, precision=highest),
            jnp.dot((q_new * q_new).T, ratio * ratio, precision=highest),
        ),
        "smp",
    )
    tiles = score.reshape(anc, traits, width)
    z_score = tiles / jnp.sqrt(info + 1e-06)[:, None, :]
    return (own_next, own_gradient / math.sqrt(width * var_count), freq_next, freq_gradient, z_score)


def solution(mesh):
    sizes = dict(mesh.shape)

    def step(genotypes, ancestry_counts, residuals, freqs):
        rows = genotypes.shape[0] // (sizes["grp"] * sizes["smp"])
        power = sizes["var"] & (sizes["var"] - 1) == 0 and sizes["var"] >= 4
        tiled = rows % (16 * sizes["var"]) == 0 and rows % (2 * LANES) == 0
        in_specs = (
            P(("grp", "smp"), "var"),
            P(("grp", "smp"), None),
            P(("grp", "smp"), None),
            P("grp", "var"),
        )
        out_specs = (
            P(("grp", "smp", "var"), None),
            P(("grp", "smp", "var"), None),
            P("grp", "var"),
            P("grp", "var"),
            P("grp", None, "var"),
        )
        return jax.shard_map(
            shards if power and tiled and sizes["smp"] == 2 else plain_shards,
            mesh=mesh,
            in_specs=in_specs,
            out_specs=out_specs,
            check_vma=False,
        )(genotypes, ancestry_counts, residuals, freqs)

    return step
```

```python
import functools
import math

import jax
import jax.numpy as jnp
from jax import lax
from jax.experimental import pallas as pl
from jax.experimental.pallas import tpu as pltpu
from jax.sharding import PartitionSpec as P


F32 = jnp.float32
BF16 = jnp.bfloat16
LANES = 128
NN = ((1,), (0,))
NT = ((1,), (1,))
TN = ((0,), (0,))


def split(x):
    high = x.astype(BF16)
    return high, (x - high.astype(F32)).astype(BF16)


def dot(a, b, dims):
    return lax.dot_general(a, b, (dims, ((), ())), preferred_element_type=F32)


def count_table(freqs):
    high, low = split(freqs)
    ones = jnp.ones_like(high)
    return jnp.concatenate(
        [
            jnp.concatenate([high, ones], axis=1),
            jnp.concatenate([low, jnp.zeros_like(ones)], axis=1),
        ],
        axis=0,
    )


def ratio_parts(counts, dosage, table):
    width = dosage.shape[1]
    both = dot(jnp.concatenate([counts, counts], axis=0), table, TN)
    recon, total = both[:, :width], both[:, width:]
    rest = total - recon
    inverse = 1.0 / (recon * rest)
    part_b = (2.0 - dosage) * recon * inverse
    part = dosage * rest * inverse - part_b
    return part, part_b, total


def half_gradient(shares, place, start, geno_ref, counts_ref, freqs, grad_ref, excess_ref, before):
    half_rows = excess_ref.shape[0]
    anc, width = freqs.shape
    table = count_table(freqs)
    for row in range(0, half_rows, LANES):
        before(row)
        first = pl.multiple_of(start + row, LANES)
        counts = counts_ref[:, pl.ds(first, LANES)].astype(F32).astype(BF16)
        dosage = geno_ref[pl.ds(first, LANES), :].astype(F32)
        part, _, total = ratio_parts(counts, dosage, table)
        high, low = split(part * total)
        excess_ref[pl.ds(row, LANES), :width] = high
        excess_ref[pl.ds(row, LANES), width:] = low
    left = jnp.concatenate(split(freqs), axis=0)
    grads = dot(jnp.concatenate([left, left], axis=1), excess_ref[...], NT)
    grads = grads[:anc] + grads[anc:]
    share = half_rows // shares
    for c in range(shares):
        grad_ref[c ^ (place % shares)] = grads[:, c * share : (c + 1) * share]


def far_kernel(
    shares, place_ref, geno_hbm, counts_hbm, freqs_hbm, grad_ref, geno_ref, counts_ref, excess_ref, freqs_ref, sems
):
    half_rows = excess_ref.shape[0]
    pieces = sems.shape[1] - 1
    size = half_rows // pieces
    place = place_ref[0]
    own_half = place // shares
    far = (1 - own_half) * half_rows
    near = own_half * half_rows

    def pair(first, count, at):
        rows = pl.ds(pl.multiple_of(first, LANES), count)
        return (
            pltpu.make_async_copy(counts_hbm.at[:, rows], counts_ref.at[:, rows], sems.at[0, at]),
            pltpu.make_async_copy(geno_hbm.at[rows, :], geno_ref.at[rows, :], sems.at[1, at]),
        )

    freqs_copy = pltpu.make_async_copy(freqs_hbm, freqs_ref, sems.at[2, 0])
    freqs_copy.start()
    moves = [pair(far + i * size, size, i) for i in range(pieces)]
    moves.append(pair(near, half_rows, pieces))
    for move in moves:
        for copy in move:
            copy.start()
    freqs_copy.wait()

    def before(row):
        if row % size == 0:
            for copy in moves[row // size]:
                copy.wait()

    half_gradient(shares, place, far, geno_ref, counts_ref, freqs_ref[...], grad_ref, excess_ref, before)
    for copy in moves[pieces]:
        copy.wait()


def near_kernel(shares, place_ref, geno_ref, counts_ref, freqs_ref, grad_ref, excess_ref):
    place = place_ref[0]
    start = (place // shares) * excess_ref.shape[0]
    half_gradient(
        shares, place, start, geno_ref, counts_ref, freqs_ref[...], grad_ref, excess_ref, lambda row: None
    )


def sums_kernel(place_ref, geno_ref, counts_ref, freqs_ref, resid_ref, sums_ref, traits_ref, own_ref, parts_ref):
    rows, width = geno_ref.shape
    table = count_table(freqs_ref[...])
    for row in range(0, rows, LANES):
        counts = counts_ref[:, pl.ds(row, LANES)].astype(F32).astype(BF16)
        dosage = geno_ref[pl.ds(row, LANES), :].astype(F32)
        part, part_b, _ = ratio_parts(counts, dosage, table)
        for at, value in enumerate((part, part_b)):
            high, low = split(value)
            parts_ref[pl.ds(row, LANES), pl.ds(at * width, width)] = high
            parts_ref[pl.ds(rows + row, LANES), pl.ds(at * width, width)] = low
    counts = counts_ref[...].astype(F32)
    left = counts.astype(BF16)
    sums_ref[...] = dot(jnp.concatenate([left, left], axis=1), parts_ref[...], NN)
    residual = resid_ref[...].astype(F32) / 1000.0
    share = traits_ref.shape[2]
    for c in range(rows // share):
        traits_ref[c] = residual[:, c * share : (c + 1) * share]
        own_ref[c] = counts[:, c * share : (c + 1) * share]


def share_kernel(variants, own_ref, counts_ref, total_ref, q_ref, grad_ref):
    gradient = total_ref[...]
    counts = counts_ref[own_ref[0]]
    fractions = counts / jnp.sum(counts, axis=0, keepdims=True)
    second = 2.0 * variants - jnp.sum(fractions * gradient, axis=0, keepdims=True)
    weighted = fractions * (gradient + second)
    q_ref[...] = weighted / jnp.sum(weighted, axis=0, keepdims=True)
    grad_ref[...] = gradient / math.sqrt(variants)


def score_kernel(shares, fresh, own_ref, *refs):
    q_refs, refs = refs[: len(shares)], refs[len(shares) :]
    geno_ref, traits_ref, freqs_ref = refs[:3]
    total_ref = None if fresh else refs[3]
    out_ref = refs[-1]
    freq_high, freq_low = split(freqs_ref[...])
    f_three = jnp.concatenate([freq_high, freq_high, freq_low], axis=0)
    anc, width = freqs_ref.shape
    traits = traits_ref.shape[1]
    score, info = None, None
    for m, q_ref in zip(shares, q_refs):
        q_new = q_ref[...]
        rows = q_new.shape[1]
        owner = own_ref[0] ^ m
        q_high, q_low = split(q_new)
        recon = dot(jnp.concatenate([q_high, q_low, q_high], axis=0), f_three, TN)
        dosage = geno_ref[pl.ds(pl.multiple_of(owner * rows, 16), rows), :].astype(F32)
        ratio = dosage / recon
        ratio_high, ratio_low = split(ratio)
        right = jnp.concatenate([ratio_high, ratio_low], axis=1)
        square_high, square_low = split(ratio * ratio)
        q2_high, q2_low = split(q_new * q_new)
        residual = traits_ref[owner]
        products = (q_new[:, None, :] * residual[None, :, :]).reshape(anc * traits, rows)
        high, low = split(products)
        wide = dot(high, right, NN)
        part = wide[:, :width] + wide[:, width:] + dot(low, ratio_high, NN)
        wide2 = dot(
            jnp.concatenate([q2_high, q2_low], axis=0),
            jnp.concatenate([square_high, square_low], axis=1),
            NN,
        )
        part2 = wide2[:anc, :width] + wide2[:anc, width:] + wide2[anc:, :width]
        score = part if score is None else score + part
        info = part2 if info is None else info + part2
    if not fresh:
        score = score + total_ref[: anc * traits]
        info = info + total_ref[anc * traits :]
    out_ref[: anc * traits] = score
    out_ref[anc * traits :] = info


def emit_kernel(
    sample_count, place_ref, q_ref, grad_ref, sums_ref, other_ref, freqs_ref, q_out, grad_out, next_out, slope_out, next_ref, slope_ref, sems
):
    _, width = freqs_ref.shape
    copies = [
        pltpu.make_async_copy(q_ref, q_out, sems.at[0]),
        pltpu.make_async_copy(grad_ref, grad_out, sems.at[1]),
    ]
    for copy in copies:
        copy.start()
    sums = sums_ref[...] + other_ref[...]
    next_ref[...], slope_ref[...] = update_freqs(
        freqs_ref[...], sums[:, :width], sums[:, width:], sample_count
    )
    copies += [
        pltpu.make_async_copy(next_ref, next_out, sems.at[2]),
        pltpu.make_async_copy(slope_ref, slope_out, sems.at[3]),
    ]
    for copy in copies[2:]:
        copy.start()
    for copy in copies:
        copy.wait()


def final_kernel(place_ref, mine_ref, other_ref, out_hbm, out_ref, sems):
    anc, traits, width = out_ref.shape
    rows = pl.ds(anc * traits, anc)
    scale = jnp.sqrt(mine_ref[rows] + other_ref[rows] + 1e-06)
    pieces = sems.shape[0]
    size = anc // pieces
    copies = []
    for i in range(pieces):
        rows = pl.ds(i * size * traits, size * traits)
        total = mine_ref[rows] + other_ref[rows]
        at = pl.ds(i * size, size)
        out_ref[at] = total.reshape(size, traits, width) / scale[i * size : (i + 1) * size, None, :]
        copies.append(pltpu.make_async_copy(out_ref.at[at], out_hbm.at[at], sems.at[i]))
        copies[-1].start()
    for copy in copies:
        copy.wait()


def update_freqs(freqs, excess_sum, second_sum, sample_count):
    allele_sum = excess_sum + second_sum
    freq_next = freqs * allele_sum / (freqs * allele_sum + (1.0 - freqs) * second_sum)
    freq_gradient = excess_sum * freqs.shape[0] / math.sqrt(sample_count)
    return (freq_next, freq_gradient)


VMEM = pltpu.VMEM
SCALARS = pl.BlockSpec(memory_space=pltpu.SMEM)
IN_VMEM = pl.BlockSpec(memory_space=pltpu.VMEM)


def call(kernel, args, outs, scratch=(), cost=2000, aliases=None, raw=()):
    specs = [SCALARS]
    held = [args[0]]
    for at, x in enumerate(args[1:], 1):
        specs.append(pl.BlockSpec(memory_space=pl.ANY) if at in raw else IN_VMEM)
        held.append(x if at in raw else pltpu.with_memory_space_constraint(x, VMEM))
    out_specs, out_shape = [], []
    for out in outs:
        if isinstance(out, jax.ShapeDtypeStruct):
            out_specs.append(pl.BlockSpec(memory_space=pltpu.HBM))
            out_shape.append(out)
        else:
            out_specs.append(IN_VMEM)
            out_shape.append(VMEM(out, F32) if isinstance(out, tuple) else out)
    return pl.pallas_call(
        kernel,
        in_specs=specs,
        out_specs=out_specs,
        out_shape=out_shape,
        scratch_shapes=list(scratch),
        input_output_aliases=aliases or {},
        cost_estimate=pl.CostEstimate(flops=cost * 400_000, bytes_accessed=0, transcendentals=0),
    )(*held)


def shards(genotypes, ancestry_counts, residuals, freqs):
    var_count = lax.axis_size("var")
    rows, width = genotypes.shape
    share = rows // var_count
    half = var_count // 2
    anc = freqs.shape[0]
    traits = residuals.shape[1]
    sample_count = rows * lax.axis_size("smp")
    variants = width * var_count
    place = lax.axis_index("var").astype(jnp.int32).reshape(1)
    dma = pltpu.SemaphoreType.DMA

    def move(x, m):
        return lax.ppermute(x, "var", [(i, i ^ m) for i in range(var_count)])

    def swap(x):
        return lax.ppermute(x, "smp", [(0, 1), (1, 0)])

    half_rows = rows // 2
    tiles = half_rows // LANES
    pieces = next(p for p in (5, 4, 3, 2, 1) if tiles % p == 0)
    excess = VMEM((half_rows, 2 * width), BF16)

    far, geno, counts = call(
        functools.partial(far_kernel, half),
        (place, genotypes, ancestry_counts.T, freqs),
        [(half, anc, share), VMEM(genotypes.shape, genotypes.dtype), VMEM((anc, rows), jnp.int32)],
        [excess, VMEM(freqs.shape, F32), dma((3, pieces + 1))],
        raw=(1, 2, 3),
    )
    (near,) = call(
        functools.partial(near_kernel, half),
        (place, geno, counts, freqs),
        [(half, anc, share)],
        [excess],
    )
    slots = {half + c: far[c] for c in range(half)}
    for m in reversed(range(half + 1, var_count, 2)):
        slots[m ^ 1] = slots[m ^ 1] + move(slots[m], 1)
    pairs = near.reshape(half // 2, 2, anc, share)
    pairs = pairs[:, 0] + move(pairs[:, 1], 1)
    slots |= {2 * c: pairs[c] for c in range(half // 2)}
    bit = 2
    while bit < var_count:
        for m in reversed(range(bit, var_count, 2 * bit)):
            slots[m ^ bit] = slots[m ^ bit] + move(slots[m], bit)
        bit *= 2

    sums, trait_parts, count_parts = call(
        sums_kernel,
        (place, geno, counts, freqs, residuals.T),
        [(anc, 2 * width), (var_count, traits, share), (var_count, anc, share)],
        [VMEM((2 * rows, 2 * width), BF16)],
    )
    sums_other = swap(sums)

    q_new, own_gradient = call(
        functools.partial(share_kernel, variants),
        (place, count_parts, slots[0]),
        [(anc, share), (anc, share)],
        cost=500,
    )

    shares = {0: q_new}
    bit = half
    while bit:
        for m in range(bit, var_count, 2 * bit):
            shares[m] = move(shares[m ^ bit], bit)
        bit //= 2

    total = None
    for m in (0, 4, 2, 1, 3, 6, 5, 7) if var_count == 8 else range(var_count):
        inputs = (geno, trait_parts, freqs) + (() if total is None else (total,))
        (total,) = call(
            functools.partial(score_kernel, (m,), total is None),
            (place, shares[m], *inputs),
            [((anc * traits + anc), width)],
            cost=700,
            aliases=None if total is None else {5: 0},
        )
    total_other = swap(total)
    out = jax.ShapeDtypeStruct
    q_out, grad_out, freq_next, freq_gradient = call(
        functools.partial(emit_kernel, sample_count),
        (place, q_new, own_gradient, sums, sums_other, freqs),
        [out((anc, share), F32)] * 2 + [out((anc, width), F32)] * 2,
        [VMEM((anc, width), F32)] * 2 + [dma((4,))],
        cost=600,
    )
    (z_score,) = call(
        final_kernel,
        (place, total, total_other),
        [out((anc, traits, width), F32)],
        [VMEM((anc, traits, width), F32), dma((4 if anc % 4 == 0 else 1,))],
        cost=300,
    )
    return (q_out.T, grad_out.T, freq_next, freq_gradient, z_score)


def plain_shards(genotypes, ancestry_counts, residuals, freqs):
    highest = lax.Precision.HIGHEST
    var_count = lax.axis_size("var")
    rows, width = genotypes.shape
    share = rows // var_count
    anc = freqs.shape[0]
    traits = residuals.shape[1]
    counts = ancestry_counts.astype(F32)
    fractions = counts / jnp.sum(counts, axis=1, keepdims=True)
    dosage = genotypes.astype(F32)
    recon = jnp.dot(fractions, freqs, precision=highest)
    ratio_a = dosage / recon
    ratio_b = (2.0 - dosage) / (1.0 - recon)
    excess = ratio_a - ratio_b
    gradient, second = lax.psum(
        (jnp.dot(excess, freqs.T, precision=highest), jnp.sum(ratio_b, axis=1)), "var"
    )
    excess_sum, second_sum = lax.psum(
        (
            jnp.dot(fractions.T, excess, precision=highest),
            jnp.dot(fractions.T, ratio_b, precision=highest),
        ),
        "smp",
    )
    freq_next, freq_gradient = update_freqs(
        freqs, excess_sum, second_sum, rows * lax.axis_size("smp")
    )
    weighted = fractions * (gradient + second[:, None])
    q_new = weighted / jnp.sum(weighted, axis=1, keepdims=True)
    first_row = lax.axis_index("var") * share
    own_next = lax.dynamic_slice_in_dim(q_new, first_row, share, 0)
    own_gradient = lax.dynamic_slice_in_dim(gradient, first_row, share, 0)
    ratio = dosage / jnp.dot(q_new, freqs, precision=highest)
    residual = residuals.astype(F32) / 1000.0
    products = (q_new[:, :, None] * residual[:, None, :]).reshape(rows, anc * traits)
    score, info = lax.psum(
        (
            jnp.dot(products.T, ratio, precision=highest),
            jnp.dot((q_new * q_new).T, ratio * ratio, precision=highest),
        ),
        "smp",
    )
    tiles = score.reshape(anc, traits, width)
    z_score = tiles / jnp.sqrt(info + 1e-06)[:, None, :]
    return (own_next, own_gradient / math.sqrt(width * var_count), freq_next, freq_gradient, z_score)


def solution(mesh):
    sizes = dict(mesh.shape)

    def step(genotypes, ancestry_counts, residuals, freqs):
        rows = genotypes.shape[0] // (sizes["grp"] * sizes["smp"])
        power = sizes["var"] & (sizes["var"] - 1) == 0 and sizes["var"] >= 4
        tiled = rows % (16 * sizes["var"]) == 0 and rows % (2 * LANES) == 0
        in_specs = (
            P(("grp", "smp"), "var"),
            P(("grp", "smp"), None),
            P(("grp", "smp"), None),
            P("grp", "var"),
        )
        out_specs = (
            P(("grp", "smp", "var"), None),
            P(("grp", "smp", "var"), None),
            P("grp", "var"),
            P("grp", "var"),
            P("grp", None, "var"),
        )
        fits = power and tiled and sizes["smp"] == 2

        def body(*args):
            return (shards if fits else plain_shards)(*args)

        mapped = jax.shard_map(
            body,
            mesh=mesh,
            in_specs=in_specs,
            out_specs=out_specs,
            check_vma=False,
        )
        return mapped(genotypes, ancestry_counts, residuals, freqs)

    return step
```

```python
import functools
import math

import jax
import jax.numpy as jnp
from jax import lax
from jax.experimental import pallas as pl
from jax.experimental.pallas import tpu as pltpu
from jax.sharding import PartitionSpec as P


F32 = jnp.float32
BF16 = jnp.bfloat16
LANES = 128
NN = ((1,), (0,))
NT = ((1,), (1,))
TN = ((0,), (0,))


def split(x):
    high = x.astype(BF16)
    return high, (x - high.astype(F32)).astype(BF16)


def dot(a, b, dims):
    return lax.dot_general(a, b, (dims, ((), ())), preferred_element_type=F32)


def count_table(freqs):
    high, low = split(freqs)
    ones = jnp.ones_like(high)
    return jnp.concatenate(
        [
            jnp.concatenate([high, ones], axis=1),
            jnp.concatenate([low, jnp.zeros_like(ones)], axis=1),
        ],
        axis=0,
    )


def ratio_parts(counts, dosage, table):
    width = dosage.shape[1]
    both = dot(jnp.concatenate([counts, counts], axis=0), table, TN)
    recon, total = both[:, :width], both[:, width:]
    rest = total - recon
    inverse = 1.0 / (recon * rest)
    part_b = (2.0 - dosage) * recon * inverse
    part = dosage * rest * inverse - part_b
    return part, part_b, total


def half_gradient(shares, place, start, geno_ref, counts_ref, freqs, grad_ref, excess_ref, before):
    half_rows = excess_ref.shape[0]
    anc, width = freqs.shape
    table = count_table(freqs)
    for row in range(0, half_rows, LANES):
        before(row)
        first = pl.multiple_of(start + row, LANES)
        counts = counts_ref[:, pl.ds(first, LANES)].astype(F32).astype(BF16)
        dosage = geno_ref[pl.ds(first, LANES), :].astype(F32)
        part, _, total = ratio_parts(counts, dosage, table)
        high, low = split(part * total)
        excess_ref[pl.ds(row, LANES), :width] = high
        excess_ref[pl.ds(row, LANES), width:] = low
    left = jnp.concatenate(split(freqs), axis=0)
    grads = dot(jnp.concatenate([left, left], axis=1), excess_ref[...], NT)
    grads = grads[:anc] + grads[anc:]
    share = half_rows // shares
    for c in range(shares):
        grad_ref[c ^ (place % shares)] = grads[:, c * share : (c + 1) * share]


def far_kernel(
    shares, place_ref, geno_hbm, counts_hbm, freqs_hbm, grad_ref, geno_ref, counts_ref, excess_ref, freqs_ref, sems
):
    half_rows = excess_ref.shape[0]
    pieces = sems.shape[1] - 1
    size = half_rows // pieces
    place = place_ref[0]
    own_half = place // shares
    far = (1 - own_half) * half_rows
    near = own_half * half_rows

    def pair(first, count, at):
        rows = pl.ds(pl.multiple_of(first, LANES), count)
        return (
            pltpu.make_async_copy(counts_hbm.at[:, rows], counts_ref.at[:, rows], sems.at[0, at]),
            pltpu.make_async_copy(geno_hbm.at[rows, :], geno_ref.at[rows, :], sems.at[1, at]),
        )

    freqs_copy = pltpu.make_async_copy(freqs_hbm, freqs_ref, sems.at[2, 0])
    freqs_copy.start()
    moves = [pair(far + i * size, size, i) for i in range(pieces)]
    moves.append(pair(near, half_rows, pieces))
    for move in moves:
        for copy in move:
            copy.start()
    freqs_copy.wait()

    def before(row):
        if row % size == 0:
            for copy in moves[row // size]:
                copy.wait()

    half_gradient(shares, place, far, geno_ref, counts_ref, freqs_ref[...], grad_ref, excess_ref, before)
    for copy in moves[pieces]:
        copy.wait()


def near_kernel(shares, place_ref, geno_ref, counts_ref, freqs_ref, grad_ref, excess_ref):
    place = place_ref[0]
    start = (place // shares) * excess_ref.shape[0]
    half_gradient(
        shares, place, start, geno_ref, counts_ref, freqs_ref[...], grad_ref, excess_ref, lambda row: None
    )


def sums_kernel(place_ref, geno_ref, counts_ref, freqs_ref, resid_ref, sums_ref, traits_ref, own_ref, parts_ref):
    rows, width = geno_ref.shape
    table = count_table(freqs_ref[...])
    for row in range(0, rows, LANES):
        counts = counts_ref[:, pl.ds(row, LANES)].astype(F32).astype(BF16)
        dosage = geno_ref[pl.ds(row, LANES), :].astype(F32)
        part, part_b, _ = ratio_parts(counts, dosage, table)
        for at, value in enumerate((part, part_b)):
            high, low = split(value)
            parts_ref[pl.ds(row, LANES), pl.ds(at * width, width)] = high
            parts_ref[pl.ds(rows + row, LANES), pl.ds(at * width, width)] = low
    counts = counts_ref[...].astype(F32)
    left = counts.astype(BF16)
    sums_ref[...] = dot(jnp.concatenate([left, left], axis=1), parts_ref[...], NN)
    residual = resid_ref[...].astype(F32) / 1000.0
    share = traits_ref.shape[2]
    for c in range(rows // share):
        traits_ref[c] = residual[:, c * share : (c + 1) * share]
        own_ref[c] = counts[:, c * share : (c + 1) * share]


def share_kernel(variants, own_ref, counts_ref, *refs):
    q_ref, grad_ref = refs[-2:]
    gradient = sum(part[...] for part in refs[1:-2]) + refs[0][...]
    counts = counts_ref[own_ref[0]]
    fractions = counts / jnp.sum(counts, axis=0, keepdims=True)
    second = 2.0 * variants - jnp.sum(fractions * gradient, axis=0, keepdims=True)
    weighted = fractions * (gradient + second)
    q_ref[...] = weighted / jnp.sum(weighted, axis=0, keepdims=True)
    grad_ref[...] = gradient / math.sqrt(variants)


def score_kernel(shares, fresh, own_ref, *refs):
    q_refs, refs = refs[: len(shares)], refs[len(shares) :]
    geno_ref, traits_ref, freqs_ref = refs[:3]
    total_ref = None if fresh else refs[3]
    out_ref = refs[-1]
    freq_high, freq_low = split(freqs_ref[...])
    f_three = jnp.concatenate([freq_high, freq_high, freq_low], axis=0)
    anc, width = freqs_ref.shape
    traits = traits_ref.shape[1]
    score, info = None, None
    for m, q_ref in zip(shares, q_refs):
        q_new = q_ref[...]
        rows = q_new.shape[1]
        owner = own_ref[0] ^ m
        q_high, q_low = split(q_new)
        recon = dot(jnp.concatenate([q_high, q_low, q_high], axis=0), f_three, TN)
        dosage = geno_ref[pl.ds(pl.multiple_of(owner * rows, 16), rows), :].astype(F32)
        ratio = dosage / recon
        ratio_high, ratio_low = split(ratio)
        right = jnp.concatenate([ratio_high, ratio_low], axis=1)
        square_high, square_low = split(ratio * ratio)
        q2_high, q2_low = split(q_new * q_new)
        residual = traits_ref[owner]
        products = (q_new[:, None, :] * residual[None, :, :]).reshape(anc * traits, rows)
        high, low = split(products)
        wide = dot(high, right, NN)
        part = wide[:, :width] + wide[:, width:] + dot(low, ratio_high, NN)
        wide2 = dot(
            jnp.concatenate([q2_high, q2_low], axis=0),
            jnp.concatenate([square_high, square_low], axis=1),
            NN,
        )
        part2 = wide2[:anc, :width] + wide2[:anc, width:] + wide2[anc:, :width]
        score = part if score is None else score + part
        info = part2 if info is None else info + part2
    if not fresh:
        score = score + total_ref[: anc * traits]
        info = info + total_ref[anc * traits :]
    out_ref[: anc * traits] = score
    out_ref[anc * traits :] = info


def emit_kernel(
    sample_count, place_ref, q_ref, grad_ref, sums_ref, other_ref, freqs_ref, q_out, grad_out, next_out, slope_out, next_ref, slope_ref, sems
):
    _, width = freqs_ref.shape
    copies = [
        pltpu.make_async_copy(q_ref, q_out, sems.at[0]),
        pltpu.make_async_copy(grad_ref, grad_out, sems.at[1]),
    ]
    for copy in copies:
        copy.start()
    sums = sums_ref[...] + other_ref[...]
    next_ref[...], slope_ref[...] = update_freqs(
        freqs_ref[...], sums[:, :width], sums[:, width:], sample_count
    )
    copies += [
        pltpu.make_async_copy(next_ref, next_out, sems.at[2]),
        pltpu.make_async_copy(slope_ref, slope_out, sems.at[3]),
    ]
    for copy in copies[2:]:
        copy.start()
    for copy in copies:
        copy.wait()


def final_kernel(place_ref, mine_ref, other_ref, out_hbm, out_ref, sems):
    anc, traits, width = out_ref.shape
    rows = pl.ds(anc * traits, anc)
    scale = jnp.sqrt(mine_ref[rows] + other_ref[rows] + 1e-06)
    pieces = sems.shape[0]
    size = anc // pieces
    copies = []
    for i in range(pieces):
        rows = pl.ds(i * size * traits, size * traits)
        total = mine_ref[rows] + other_ref[rows]
        at = pl.ds(i * size, size)
        out_ref[at] = total.reshape(size, traits, width) / scale[i * size : (i + 1) * size, None, :]
        copies.append(pltpu.make_async_copy(out_ref.at[at], out_hbm.at[at], sems.at[i]))
        copies[-1].start()
    for copy in copies:
        copy.wait()


def update_freqs(freqs, excess_sum, second_sum, sample_count):
    allele_sum = excess_sum + second_sum
    freq_next = freqs * allele_sum / (freqs * allele_sum + (1.0 - freqs) * second_sum)
    freq_gradient = excess_sum * freqs.shape[0] / math.sqrt(sample_count)
    return (freq_next, freq_gradient)


VMEM = pltpu.VMEM
SCALARS = pl.BlockSpec(memory_space=pltpu.SMEM)
IN_VMEM = pl.BlockSpec(memory_space=pltpu.VMEM)


def call(kernel, args, outs, scratch=(), cost=2000, aliases=None, raw=()):
    specs = [SCALARS]
    held = [args[0]]
    for at, x in enumerate(args[1:], 1):
        specs.append(pl.BlockSpec(memory_space=pl.ANY) if at in raw else IN_VMEM)
        held.append(x if at in raw else pltpu.with_memory_space_constraint(x, VMEM))
    out_specs, out_shape = [], []
    for out in outs:
        if isinstance(out, jax.ShapeDtypeStruct):
            out_specs.append(pl.BlockSpec(memory_space=pltpu.HBM))
            out_shape.append(out)
        else:
            out_specs.append(IN_VMEM)
            out_shape.append(VMEM(out, F32) if isinstance(out, tuple) else out)
    return pl.pallas_call(
        kernel,
        in_specs=specs,
        out_specs=out_specs,
        out_shape=out_shape,
        scratch_shapes=list(scratch),
        input_output_aliases=aliases or {},
        cost_estimate=pl.CostEstimate(flops=cost * 400_000, bytes_accessed=0, transcendentals=0),
    )(*held)


def shards(genotypes, ancestry_counts, residuals, freqs):
    var_count = lax.axis_size("var")
    rows, width = genotypes.shape
    share = rows // var_count
    half = var_count // 2
    anc = freqs.shape[0]
    traits = residuals.shape[1]
    sample_count = rows * lax.axis_size("smp")
    variants = width * var_count
    place = lax.axis_index("var").astype(jnp.int32).reshape(1)
    dma = pltpu.SemaphoreType.DMA

    def move(x, m):
        return lax.ppermute(x, "var", [(i, i ^ m) for i in range(var_count)])

    def swap(x):
        return lax.ppermute(x, "smp", [(0, 1), (1, 0)])

    half_rows = rows // 2
    tiles = half_rows // LANES
    pieces = next(p for p in (5, 4, 3, 2, 1) if tiles % p == 0)
    excess = VMEM((half_rows, 2 * width), BF16)

    far, geno, counts = call(
        functools.partial(far_kernel, half),
        (place, genotypes, ancestry_counts.T, freqs),
        [(half, anc, share), VMEM(genotypes.shape, genotypes.dtype), VMEM((anc, rows), jnp.int32)],
        [excess, VMEM(freqs.shape, F32), dma((3, pieces + 1))],
        raw=(1, 2, 3),
    )
    (near,) = call(
        functools.partial(near_kernel, half),
        (place, geno, counts, freqs),
        [(half, anc, share)],
        [excess],
    )
    pairs = far.reshape(half // 2, 2, anc, share)
    joined = pairs[:, 0] + move(pairs[:, 1], 1)
    arrived = [near[0]] + [move(near[m], m) for m in range(1, half)]
    arrived += [move(joined[c], half + 2 * c) for c in range(half // 2)]

    sums, trait_parts, count_parts = call(
        sums_kernel,
        (place, geno, counts, freqs, residuals.T),
        [(anc, 2 * width), (var_count, traits, share), (var_count, anc, share)],
        [VMEM((2 * rows, 2 * width), BF16)],
    )
    sums_other = swap(sums)

    q_new, own_gradient = call(
        functools.partial(share_kernel, variants),
        (place, count_parts, *arrived),
        [(anc, share), (anc, share)],
        cost=500,
    )

    shares = {0: q_new}
    for m in (*range(half, var_count, 2), *range(1, half)):
        shares[m] = move(q_new, m)
    for m in range(half + 1, var_count, 2):
        shares[m] = move(shares[m - 1], 1)

    total = None
    for m in (0, 2, 1, 4, 3, 6, 5, 7) if var_count == 8 else range(var_count):
        inputs = (geno, trait_parts, freqs) + (() if total is None else (total,))
        (total,) = call(
            functools.partial(score_kernel, (m,), total is None),
            (place, shares[m], *inputs),
            [((anc * traits + anc), width)],
            cost=700,
            aliases=None if total is None else {5: 0},
        )
    total_other = swap(total)
    out = jax.ShapeDtypeStruct
    q_out, grad_out, freq_next, freq_gradient = call(
        functools.partial(emit_kernel, sample_count),
        (place, q_new, own_gradient, sums, sums_other, freqs),
        [out((anc, share), F32)] * 2 + [out((anc, width), F32)] * 2,
        [VMEM((anc, width), F32)] * 2 + [dma((4,))],
        cost=600,
    )
    (z_score,) = call(
        final_kernel,
        (place, total, total_other),
        [out((anc, traits, width), F32)],
        [VMEM((anc, traits, width), F32), dma((4 if anc % 4 == 0 else 1,))],
        cost=300,
    )
    return (q_out.T, grad_out.T, freq_next, freq_gradient, z_score)


def plain_shards(genotypes, ancestry_counts, residuals, freqs):
    highest = lax.Precision.HIGHEST
    var_count = lax.axis_size("var")
    rows, width = genotypes.shape
    share = rows // var_count
    anc = freqs.shape[0]
    traits = residuals.shape[1]
    counts = ancestry_counts.astype(F32)
    fractions = counts / jnp.sum(counts, axis=1, keepdims=True)
    dosage = genotypes.astype(F32)
    recon = jnp.dot(fractions, freqs, precision=highest)
    ratio_a = dosage / recon
    ratio_b = (2.0 - dosage) / (1.0 - recon)
    excess = ratio_a - ratio_b
    gradient, second = lax.psum(
        (jnp.dot(excess, freqs.T, precision=highest), jnp.sum(ratio_b, axis=1)), "var"
    )
    excess_sum, second_sum = lax.psum(
        (
            jnp.dot(fractions.T, excess, precision=highest),
            jnp.dot(fractions.T, ratio_b, precision=highest),
        ),
        "smp",
    )
    freq_next, freq_gradient = update_freqs(
        freqs, excess_sum, second_sum, rows * lax.axis_size("smp")
    )
    weighted = fractions * (gradient + second[:, None])
    q_new = weighted / jnp.sum(weighted, axis=1, keepdims=True)
    first_row = lax.axis_index("var") * share
    own_next = lax.dynamic_slice_in_dim(q_new, first_row, share, 0)
    own_gradient = lax.dynamic_slice_in_dim(gradient, first_row, share, 0)
    ratio = dosage / jnp.dot(q_new, freqs, precision=highest)
    residual = residuals.astype(F32) / 1000.0
    products = (q_new[:, :, None] * residual[:, None, :]).reshape(rows, anc * traits)
    score, info = lax.psum(
        (
            jnp.dot(products.T, ratio, precision=highest),
            jnp.dot((q_new * q_new).T, ratio * ratio, precision=highest),
        ),
        "smp",
    )
    tiles = score.reshape(anc, traits, width)
    z_score = tiles / jnp.sqrt(info + 1e-06)[:, None, :]
    return (own_next, own_gradient / math.sqrt(width * var_count), freq_next, freq_gradient, z_score)


def solution(mesh):
    sizes = dict(mesh.shape)

    def step(genotypes, ancestry_counts, residuals, freqs):
        rows = genotypes.shape[0] // (sizes["grp"] * sizes["smp"])
        power = sizes["var"] & (sizes["var"] - 1) == 0 and sizes["var"] >= 4
        tiled = rows % (16 * sizes["var"]) == 0 and rows % (2 * LANES) == 0
        in_specs = (
            P(("grp", "smp"), "var"),
            P(("grp", "smp"), None),
            P(("grp", "smp"), None),
            P("grp", "var"),
        )
        out_specs = (
            P(("grp", "smp", "var"), None),
            P(("grp", "smp", "var"), None),
            P("grp", "var"),
            P("grp", "var"),
            P("grp", None, "var"),
        )
        fits = power and tiled and sizes["smp"] == 2

        def body(*args):
            return (shards if fits else plain_shards)(*args)

        mapped = jax.shard_map(
            body,
            mesh=mesh,
            in_specs=in_specs,
            out_specs=out_specs,
            check_vma=False,
        )
        return mapped(genotypes, ancestry_counts, residuals, freqs)

    return step
```

```python
import functools
import math

import jax
import jax.numpy as jnp
from jax import lax
from jax.experimental import pallas as pl
from jax.experimental.pallas import tpu as pltpu
from jax.sharding import PartitionSpec as P


F32 = jnp.float32
BF16 = jnp.bfloat16
LANES = 128
NN = ((1,), (0,))
NT = ((1,), (1,))
TN = ((0,), (0,))


def split(x):
    high = x.astype(BF16)
    return high, (x - high.astype(F32)).astype(BF16)


def dot(a, b, dims):
    return lax.dot_general(a, b, (dims, ((), ())), preferred_element_type=F32)


def count_table(freqs):
    high, low = split(freqs)
    ones = jnp.ones_like(high)
    return jnp.concatenate(
        [
            jnp.concatenate([high, ones], axis=1),
            jnp.concatenate([low, jnp.zeros_like(ones)], axis=1),
        ],
        axis=0,
    )


def ratio_parts(counts, dosage, table):
    width = dosage.shape[1]
    both = dot(jnp.concatenate([counts, counts], axis=0), table, TN)
    recon, total = both[:, :width], both[:, width:]
    inverse = 1.0 / (recon * (total - recon))
    part = (dosage * total - (recon + recon)) * inverse
    return part, recon, inverse, total


def half_gradient(shares, place, start, geno_ref, counts_ref, freqs, grad_ref, excess_ref, before):
    half_rows = excess_ref.shape[0]
    anc, width = freqs.shape
    table = count_table(freqs)
    for row in range(0, half_rows, LANES):
        before(row)
        first = pl.multiple_of(start + row, LANES)
        counts = counts_ref[:, pl.ds(first, LANES)].astype(F32).astype(BF16)
        dosage = geno_ref[pl.ds(first, LANES), :].astype(F32)
        part, _, _, total = ratio_parts(counts, dosage, table)
        high, low = split(part * total)
        excess_ref[pl.ds(row, LANES), :width] = high
        excess_ref[pl.ds(row, LANES), width:] = low
    left = jnp.concatenate(split(freqs), axis=0)
    grads = dot(jnp.concatenate([left, left], axis=1), excess_ref[...], NT)
    grads = grads[:anc] + grads[anc:]
    share = half_rows // shares
    for c in range(shares):
        grad_ref[c ^ (place % shares)] = grads[:, c * share : (c + 1) * share]


def far_kernel(
    shares, place_ref, geno_hbm, counts_hbm, freqs_hbm, grad_ref, geno_ref, counts_ref, excess_ref, freqs_ref, sems
):
    half_rows = excess_ref.shape[0]
    pieces = sems.shape[1] - 1
    size = half_rows // pieces
    place = place_ref[0]
    own_half = place // shares
    far = (1 - own_half) * half_rows
    near = own_half * half_rows

    def pair(first, count, at):
        rows = pl.ds(pl.multiple_of(first, LANES), count)
        return (
            pltpu.make_async_copy(counts_hbm.at[:, rows], counts_ref.at[:, rows], sems.at[0, at]),
            pltpu.make_async_copy(geno_hbm.at[rows, :], geno_ref.at[rows, :], sems.at[1, at]),
        )

    freqs_copy = pltpu.make_async_copy(freqs_hbm, freqs_ref, sems.at[2, 0])
    freqs_copy.start()
    moves = [pair(far + i * size, size, i) for i in range(pieces)]
    moves.append(pair(near, half_rows, pieces))
    for move in moves[:pieces]:
        for copy in move:
            copy.start()
    freqs_copy.wait()

    def before(row):
        if row % size == 0:
            for copy in moves[row // size]:
                copy.wait()
        if row == half_rows // 2 // size * size:
            for copy in moves[pieces]:
                copy.start()

    half_gradient(shares, place, far, geno_ref, counts_ref, freqs_ref[...], grad_ref, excess_ref, before)
    for copy in moves[pieces]:
        copy.wait()


def near_kernel(shares, place_ref, geno_ref, counts_ref, freqs_ref, grad_ref, excess_ref):
    place = place_ref[0]
    start = (place // shares) * excess_ref.shape[0]
    half_gradient(
        shares, place, start, geno_ref, counts_ref, freqs_ref[...], grad_ref, excess_ref, lambda row: None
    )


def sums_kernel(first, place_ref, geno_ref, counts_ref, freqs_ref, *refs):
    other_ref, refs = refs[0], refs[1:]
    sums_ref, parts_ref = refs[0], refs[-1]
    half_rows = parts_ref.shape[0] // 2
    width = freqs_ref.shape[1]
    start = 0 if first else half_rows
    table = count_table(freqs_ref[...])
    for row in range(0, half_rows, LANES):
        counts = counts_ref[:, pl.ds(start + row, LANES)].astype(F32).astype(BF16)
        dosage = geno_ref[pl.ds(start + row, LANES), :].astype(F32)
        part, recon, inverse, _ = ratio_parts(counts, dosage, table)
        for at, value in enumerate((part, (2.0 - dosage) * (recon * inverse))):
            high, low = split(value)
            parts_ref[pl.ds(row, LANES), pl.ds(at * width, width)] = high
            parts_ref[pl.ds(half_rows + row, LANES), pl.ds(at * width, width)] = low
    left = counts_ref[:, pl.ds(start, half_rows)].astype(F32).astype(BF16)
    sums = dot(jnp.concatenate([left, left], axis=1), parts_ref[...], NN)
    if not first:
        sums_ref[...] = sums + other_ref[...]
        return
    sums_ref[...] = sums
    traits_ref, own_ref = refs[1:3]
    residual = other_ref[...].astype(F32) / 1000.0
    counts = counts_ref[...].astype(F32)
    share = traits_ref.shape[2]
    for c in range(traits_ref.shape[0]):
        traits_ref[c] = residual[:, c * share : (c + 1) * share]
        own_ref[c] = counts[:, c * share : (c + 1) * share]


def share_kernel(variants, own_ref, counts_ref, *refs):
    q_ref, grad_ref = refs[-2:]
    gradient = sum(part[...] for part in refs[1:-2]) + refs[0][...]
    counts = counts_ref[own_ref[0]]
    fractions = counts / jnp.sum(counts, axis=0, keepdims=True)
    second = 2.0 * variants - jnp.sum(fractions * gradient, axis=0, keepdims=True)
    weighted = fractions * (gradient + second)
    q_ref[...] = weighted / jnp.sum(weighted, axis=0, keepdims=True)
    grad_ref[...] = gradient / math.sqrt(variants)


def score_kernel(shares, fresh, own_ref, *refs):
    q_refs, refs = refs[: len(shares)], refs[len(shares) :]
    geno_ref, traits_ref, freqs_ref = refs[:3]
    total_ref = None if fresh else refs[3]
    out_ref = refs[-1]
    freq_high, freq_low = split(freqs_ref[...])
    f_three = jnp.concatenate([freq_high, freq_high, freq_low], axis=0)
    anc, width = freqs_ref.shape
    traits = traits_ref.shape[1]
    score, info = None, None
    for m, q_ref in zip(shares, q_refs):
        q_new = q_ref[...]
        rows = q_new.shape[1]
        owner = own_ref[0] ^ m
        q_high, q_low = split(q_new)
        recon = dot(jnp.concatenate([q_high, q_low, q_high], axis=0), f_three, TN)
        dosage = geno_ref[pl.ds(pl.multiple_of(owner * rows, 16), rows), :].astype(F32)
        ratio = dosage / recon
        ratio_high, ratio_low = split(ratio)
        right = jnp.concatenate([ratio_high, ratio_low], axis=1)
        square_high, square_low = split(ratio * ratio)
        q2_high, q2_low = split(q_new * q_new)
        residual = traits_ref[owner]
        products = (q_new[:, None, :] * residual[None, :, :]).reshape(anc * traits, rows)
        high, low = split(products)
        wide = dot(high, right, NN)
        part = wide[:, :width] + wide[:, width:] + dot(low, ratio_high, NN)
        wide2 = dot(
            jnp.concatenate([q2_high, q2_low], axis=0),
            jnp.concatenate([square_high, square_low], axis=1),
            NN,
        )
        part2 = wide2[:anc, :width] + wide2[:anc, width:] + wide2[anc:, :width]
        score = part if score is None else score + part
        info = part2 if info is None else info + part2
    if not fresh:
        score = score + total_ref[: anc * traits]
        info = info + total_ref[anc * traits :]
    out_ref[: anc * traits] = score
    out_ref[anc * traits :] = info


def emit_kernel(
    sample_count, place_ref, q_ref, grad_ref, sums_ref, other_ref, freqs_ref, q_out, grad_out, next_out, slope_out, next_ref, slope_ref, sems
):
    _, width = freqs_ref.shape
    copies = [
        pltpu.make_async_copy(q_ref, q_out, sems.at[0]),
        pltpu.make_async_copy(grad_ref, grad_out, sems.at[1]),
    ]
    for copy in copies:
        copy.start()
    sums = sums_ref[...] + other_ref[...]
    next_ref[...], slope_ref[...] = update_freqs(
        freqs_ref[...], sums[:, :width], sums[:, width:], sample_count
    )
    copies += [
        pltpu.make_async_copy(next_ref, next_out, sems.at[2]),
        pltpu.make_async_copy(slope_ref, slope_out, sems.at[3]),
    ]
    for copy in copies[2:]:
        copy.start()
    for copy in copies:
        copy.wait()


def final_kernel(place_ref, mine_ref, other_ref, out_hbm, out_ref, sems):
    anc, traits, width = out_ref.shape
    rows = pl.ds(anc * traits, anc)
    scale = jnp.sqrt(mine_ref[rows] + other_ref[rows] + 1e-06)
    pieces = sems.shape[0]
    size = anc // pieces
    copies = []
    for i in range(pieces):
        rows = pl.ds(i * size * traits, size * traits)
        total = mine_ref[rows] + other_ref[rows]
        at = pl.ds(i * size, size)
        out_ref[at] = total.reshape(size, traits, width) / scale[i * size : (i + 1) * size, None, :]
        copies.append(pltpu.make_async_copy(out_ref.at[at], out_hbm.at[at], sems.at[i]))
        copies[-1].start()
    for copy in copies:
        copy.wait()


def update_freqs(freqs, excess_sum, second_sum, sample_count):
    allele_sum = excess_sum + second_sum
    freq_next = freqs * allele_sum / (freqs * allele_sum + (1.0 - freqs) * second_sum)
    freq_gradient = excess_sum * freqs.shape[0] / math.sqrt(sample_count)
    return (freq_next, freq_gradient)


VMEM = pltpu.VMEM
SCALARS = pl.BlockSpec(memory_space=pltpu.SMEM)
IN_VMEM = pl.BlockSpec(memory_space=pltpu.VMEM)


def call(kernel, args, outs, scratch=(), cost=2000, aliases=None, raw=()):
    specs = [SCALARS]
    held = [args[0]]
    for at, x in enumerate(args[1:], 1):
        specs.append(pl.BlockSpec(memory_space=pl.ANY) if at in raw else IN_VMEM)
        held.append(x if at in raw else pltpu.with_memory_space_constraint(x, VMEM))
    out_specs, out_shape = [], []
    for out in outs:
        if isinstance(out, jax.ShapeDtypeStruct):
            out_specs.append(pl.BlockSpec(memory_space=pltpu.HBM))
            out_shape.append(out)
        else:
            out_specs.append(IN_VMEM)
            out_shape.append(VMEM(out, F32) if isinstance(out, tuple) else out)
    return pl.pallas_call(
        kernel,
        in_specs=specs,
        out_specs=out_specs,
        out_shape=out_shape,
        scratch_shapes=list(scratch),
        input_output_aliases=aliases or {},
        cost_estimate=pl.CostEstimate(flops=cost * 400_000, bytes_accessed=0, transcendentals=0),
    )(*held)


def shards(genotypes, ancestry_counts, residuals, freqs):
    var_count = lax.axis_size("var")
    rows, width = genotypes.shape
    share = rows // var_count
    half = var_count // 2
    anc = freqs.shape[0]
    traits = residuals.shape[1]
    sample_count = rows * lax.axis_size("smp")
    variants = width * var_count
    place = lax.axis_index("var").astype(jnp.int32).reshape(1)
    dma = pltpu.SemaphoreType.DMA

    def move(x, m):
        return lax.ppermute(x, "var", [(i, i ^ m) for i in range(var_count)])

    def swap(x):
        return lax.ppermute(x, "smp", [(0, 1), (1, 0)])

    half_rows = rows // 2
    tiles = half_rows // LANES
    pieces = next(p for p in (5, 4, 3, 2, 1) if tiles % p == 0)
    excess = VMEM((half_rows, 2 * width), BF16)

    far, geno, counts = call(
        functools.partial(far_kernel, half),
        (place, genotypes, ancestry_counts.T, freqs),
        [(half, anc, share), VMEM(genotypes.shape, genotypes.dtype), VMEM((anc, rows), jnp.int32)],
        [excess, VMEM(freqs.shape, F32), dma((3, pieces + 1))],
        raw=(1, 2, 3),
    )
    (near,) = call(
        functools.partial(near_kernel, half),
        (place, geno, counts, freqs),
        [(half, anc, share)],
        [excess],
    )
    pairs = far.reshape(half // 2, 2, anc, share)
    joined = pairs[:, 0] + move(pairs[:, 1], 1)
    arrived = [near[0]] + [move(near[m], m) for m in range(1, half)]
    arrived += [move(joined[c], half + 2 * c) for c in range(half // 2)]

    halves = VMEM((rows, 2 * width), BF16)
    sums, trait_parts, count_parts = call(
        functools.partial(sums_kernel, True),
        (place, geno, counts, freqs, residuals.T),
        [(anc, 2 * width), (var_count, traits, share), (var_count, anc, share)],
        [halves],
        cost=1200,
    )
    (sums,) = call(
        functools.partial(sums_kernel, False),
        (place, geno, counts, freqs, sums),
        [(anc, 2 * width)],
        [halves],
        cost=1000,
    )
    sums_other = swap(sums)

    q_new, own_gradient = call(
        functools.partial(share_kernel, variants),
        (place, count_parts, *arrived),
        [(anc, share), (anc, share)],
        cost=500,
    )

    shares = {0: q_new}
    for m in (*range(half, var_count, 2), *range(2, half, 2), 1):
        shares[m] = move(q_new, m)
    early = range(2, var_count - 2, 2)
    passed = move(jnp.stack([shares[m] for m in early]), 1)
    for at, m in enumerate(early):
        shares[m + 1] = passed[at]
    shares[var_count - 1] = move(shares[var_count - 2], 1)

    total = None
    for m in (0, 2, 1, 4, 6, 3, 5, 7) if var_count == 8 else range(var_count):
        inputs = (geno, trait_parts, freqs) + (() if total is None else (total,))
        (total,) = call(
            functools.partial(score_kernel, (m,), total is None),
            (place, shares[m], *inputs),
            [((anc * traits + anc), width)],
            cost=700,
            aliases=None if total is None else {5: 0},
        )
    total_other = swap(total)
    out = jax.ShapeDtypeStruct
    q_out, grad_out, freq_next, freq_gradient = call(
        functools.partial(emit_kernel, sample_count),
        (place, q_new, own_gradient, sums, sums_other, freqs),
        [out((anc, share), F32)] * 2 + [out((anc, width), F32)] * 2,
        [VMEM((anc, width), F32)] * 2 + [dma((4,))],
        cost=600,
    )
    (z_score,) = call(
        final_kernel,
        (place, total, total_other),
        [out((anc, traits, width), F32)],
        [VMEM((anc, traits, width), F32), dma((4 if anc % 4 == 0 else 1,))],
        cost=300,
    )
    return (q_out.T, grad_out.T, freq_next, freq_gradient, z_score)


def plain_shards(genotypes, ancestry_counts, residuals, freqs):
    highest = lax.Precision.HIGHEST
    var_count = lax.axis_size("var")
    rows, width = genotypes.shape
    share = rows // var_count
    anc = freqs.shape[0]
    traits = residuals.shape[1]
    counts = ancestry_counts.astype(F32)
    fractions = counts / jnp.sum(counts, axis=1, keepdims=True)
    dosage = genotypes.astype(F32)
    recon = jnp.dot(fractions, freqs, precision=highest)
    ratio_a = dosage / recon
    ratio_b = (2.0 - dosage) / (1.0 - recon)
    excess = ratio_a - ratio_b
    gradient, second = lax.psum(
        (jnp.dot(excess, freqs.T, precision=highest), jnp.sum(ratio_b, axis=1)), "var"
    )
    excess_sum, second_sum = lax.psum(
        (
            jnp.dot(fractions.T, excess, precision=highest),
            jnp.dot(fractions.T, ratio_b, precision=highest),
        ),
        "smp",
    )
    freq_next, freq_gradient = update_freqs(
        freqs, excess_sum, second_sum, rows * lax.axis_size("smp")
    )
    weighted = fractions * (gradient + second[:, None])
    q_new = weighted / jnp.sum(weighted, axis=1, keepdims=True)
    first_row = lax.axis_index("var") * share
    own_next = lax.dynamic_slice_in_dim(q_new, first_row, share, 0)
    own_gradient = lax.dynamic_slice_in_dim(gradient, first_row, share, 0)
    ratio = dosage / jnp.dot(q_new, freqs, precision=highest)
    residual = residuals.astype(F32) / 1000.0
    products = (q_new[:, :, None] * residual[:, None, :]).reshape(rows, anc * traits)
    score, info = lax.psum(
        (
            jnp.dot(products.T, ratio, precision=highest),
            jnp.dot((q_new * q_new).T, ratio * ratio, precision=highest),
        ),
        "smp",
    )
    tiles = score.reshape(anc, traits, width)
    z_score = tiles / jnp.sqrt(info + 1e-06)[:, None, :]
    return (own_next, own_gradient / math.sqrt(width * var_count), freq_next, freq_gradient, z_score)


def solution(mesh):
    sizes = dict(mesh.shape)

    def step(genotypes, ancestry_counts, residuals, freqs):
        rows = genotypes.shape[0] // (sizes["grp"] * sizes["smp"])
        power = sizes["var"] & (sizes["var"] - 1) == 0 and sizes["var"] >= 4
        tiled = rows % (16 * sizes["var"]) == 0 and rows % (2 * LANES) == 0
        in_specs = (
            P(("grp", "smp"), "var"),
            P(("grp", "smp"), None),
            P(("grp", "smp"), None),
            P("grp", "var"),
        )
        out_specs = (
            P(("grp", "smp", "var"), None),
            P(("grp", "smp", "var"), None),
            P("grp", "var"),
            P("grp", "var"),
            P("grp", None, "var"),
        )
        fits = power and tiled and sizes["smp"] == 2

        def body(*args):
            return (shards if fits else plain_shards)(*args)

        mapped = jax.shard_map(
            body,
            mesh=mesh,
            in_specs=in_specs,
            out_specs=out_specs,
            check_vma=False,
        )
        return mapped(genotypes, ancestry_counts, residuals, freqs)

    return step
```

```python
import functools
import math

import jax
import jax.numpy as jnp
from jax import lax
from jax.experimental import pallas as pl
from jax.experimental.pallas import tpu as pltpu
from jax.sharding import PartitionSpec as P


F32 = jnp.float32
BF16 = jnp.bfloat16
LANES = 128
VMEM_LIMIT = 60 * 1024 * 1024
NN = ((1,), (0,))
NT = ((1,), (1,))
TN = ((0,), (0,))


def split(x):
    high = x.astype(BF16)
    return high, (x - high.astype(F32)).astype(BF16)


def dot(a, b, dims):
    return lax.dot_general(a, b, (dims, ((), ())), preferred_element_type=F32)


def count_table(freqs):
    high, low = split(freqs)
    ones = jnp.ones_like(high)
    return jnp.concatenate(
        [
            jnp.concatenate([high, ones], axis=1),
            jnp.concatenate([low, jnp.zeros_like(ones)], axis=1),
        ],
        axis=0,
    )


def ratio_parts(counts, dosage, table):
    width = dosage.shape[1]
    both = dot(jnp.concatenate([counts, counts], axis=0), table, TN)
    recon, total = both[:, :width], both[:, width:]
    inverse = 1.0 / (recon * (total - recon))
    part = (dosage * total - (recon + recon)) * inverse
    return part, recon, inverse, total


def half_gradient(shares, place, start, geno_ref, counts_ref, freqs, grad_ref, excess_ref, before):
    half_rows = excess_ref.shape[0]
    anc, width = freqs.shape
    table = count_table(freqs)
    for row in range(0, half_rows, LANES):
        before(row)
        first = pl.multiple_of(start + row, LANES)
        counts = counts_ref[:, pl.ds(first, LANES)].astype(F32).astype(BF16)
        dosage = geno_ref[pl.ds(first, LANES), :].astype(F32)
        part, _, _, total = ratio_parts(counts, dosage, table)
        high, low = split(part * total)
        excess_ref[pl.ds(row, LANES), :width] = high
        excess_ref[pl.ds(row, LANES), width:] = low
    left = jnp.concatenate(split(freqs), axis=0)
    grads = dot(jnp.concatenate([left, left], axis=1), excess_ref[...], NT)
    grads = grads[:anc] + grads[anc:]
    share = half_rows // shares
    for c in range(shares):
        grad_ref[c ^ (place % shares)] = grads[:, c * share : (c + 1) * share]


def far_kernel(
    shares, place_ref, geno_hbm, counts_hbm, freqs_hbm, grad_ref, geno_ref, counts_ref, excess_ref, freqs_ref, sems
):
    half_rows = excess_ref.shape[0]
    pieces = sems.shape[1] - 1
    size = half_rows // pieces
    place = place_ref[0]
    own_half = place // shares
    far = (1 - own_half) * half_rows
    near = own_half * half_rows

    def pair(first, count, at):
        rows = pl.ds(pl.multiple_of(first, LANES), count)
        return (
            pltpu.make_async_copy(counts_hbm.at[:, rows], counts_ref.at[:, rows], sems.at[0, at]),
            pltpu.make_async_copy(geno_hbm.at[rows, :], geno_ref.at[rows, :], sems.at[1, at]),
        )

    freqs_copy = pltpu.make_async_copy(freqs_hbm, freqs_ref, sems.at[2, 0])
    freqs_copy.start()
    moves = [pair(far + i * size, size, i) for i in range(pieces)]
    moves.append(pair(near, half_rows, pieces))
    for move in moves[:pieces]:
        for copy in move:
            copy.start()
    freqs_copy.wait()

    def before(row):
        if row % size == 0:
            for copy in moves[row // size]:
                copy.wait()
        if row == half_rows // 2 // size * size:
            for copy in moves[pieces]:
                copy.start()

    half_gradient(shares, place, far, geno_ref, counts_ref, freqs_ref[...], grad_ref, excess_ref, before)
    for copy in moves[pieces]:
        copy.wait()


def near_kernel(shares, place_ref, geno_ref, counts_ref, freqs_ref, grad_ref, excess_ref):
    place = place_ref[0]
    start = (place // shares) * excess_ref.shape[0]
    half_gradient(
        shares, place, start, geno_ref, counts_ref, freqs_ref[...], grad_ref, excess_ref, lambda row: None
    )


def sums_kernel(first, place_ref, geno_ref, counts_ref, freqs_ref, *refs):
    other_ref, refs = refs[0], refs[1:]
    sums_ref, parts_ref = refs[0], refs[-1]
    half_rows = parts_ref.shape[0] // 2
    width = freqs_ref.shape[1]
    start = 0 if first else half_rows
    table = count_table(freqs_ref[...])
    for row in range(0, half_rows, LANES):
        counts = counts_ref[:, pl.ds(start + row, LANES)].astype(F32).astype(BF16)
        dosage = geno_ref[pl.ds(start + row, LANES), :].astype(F32)
        part, recon, inverse, _ = ratio_parts(counts, dosage, table)
        for at, value in enumerate((part, (2.0 - dosage) * (recon * inverse))):
            high, low = split(value)
            parts_ref[pl.ds(row, LANES), pl.ds(at * width, width)] = high
            parts_ref[pl.ds(half_rows + row, LANES), pl.ds(at * width, width)] = low
    left = counts_ref[:, pl.ds(start, half_rows)].astype(F32).astype(BF16)
    sums = dot(jnp.concatenate([left, left], axis=1), parts_ref[...], NN)
    if not first:
        sums_ref[...] = sums + other_ref[...]
        return
    sums_ref[...] = sums
    traits_ref, own_ref = refs[1:3]
    residual = other_ref[...].astype(F32) / 1000.0
    counts = counts_ref[...].astype(F32)
    share = traits_ref.shape[2]
    for c in range(traits_ref.shape[0]):
        traits_ref[c] = residual[:, c * share : (c + 1) * share]
        own_ref[c] = counts[:, c * share : (c + 1) * share]


def share_kernel(variants, own_ref, counts_ref, *refs):
    q_ref, grad_ref = refs[-2:]
    gradient = sum(part[...] for part in refs[1:-2]) + refs[0][...]
    counts = counts_ref[own_ref[0]]
    fractions = counts / jnp.sum(counts, axis=0, keepdims=True)
    second = 2.0 * variants - jnp.sum(fractions * gradient, axis=0, keepdims=True)
    weighted = fractions * (gradient + second)
    q_ref[...] = weighted / jnp.sum(weighted, axis=0, keepdims=True)
    grad_ref[...] = gradient / math.sqrt(variants)


def score_kernel(shares, fresh, own_ref, *refs):
    q_refs, refs = refs[: len(shares)], refs[len(shares) :]
    geno_ref, traits_ref, freqs_ref = refs[:3]
    out_ref = refs[-2]
    freq_high, freq_low = split(freqs_ref[...])
    f_three = jnp.concatenate([freq_high, freq_high, freq_low], axis=0)
    anc, width = freqs_ref.shape
    traits = traits_ref.shape[1]
    for m, q_ref in zip(shares, q_refs):
        q_new = q_ref[...]
        rows = q_new.shape[1]
        owner = own_ref[0] ^ m
        q_high, q_low = split(q_new)
        recon = dot(jnp.concatenate([q_high, q_low, q_high], axis=0), f_three, TN)
        dosage = geno_ref[pl.ds(pl.multiple_of(owner * rows, 16), rows), :].astype(F32)
        ratio = dosage / recon
        ratio_high, ratio_low = split(ratio)
        right = jnp.concatenate([ratio_high, ratio_low], axis=1)
        square_high, square_low = split(ratio * ratio)
        q2_high, q2_low = split(q_new * q_new)
        residual = traits_ref[owner]
        products = (q_new[:, None, :] * residual[None, :, :]).reshape(anc * traits, rows)
        high, low = split(products)
        wide = dot(high, right, NN)
        part = wide[:, :width] + wide[:, width:] + dot(low, ratio_high, NN)
        wide2 = dot(
            jnp.concatenate([q2_high, q2_low], axis=0),
            jnp.concatenate([square_high, square_low], axis=1),
            NN,
        )
        part2 = wide2[:anc, :width] + wide2[:anc, width:] + wide2[anc:, :width]
        if fresh and m == shares[0]:
            out_ref[: anc * traits] = part
            out_ref[anc * traits :] = part2
        else:
            out_ref[: anc * traits] += part
            out_ref[anc * traits :] += part2


def emit_kernel(
    sample_count, place_ref, q_ref, grad_ref, sums_ref, other_ref, freqs_ref, q_out, grad_out, next_out, slope_out, next_ref, slope_ref, sems
):
    _, width = freqs_ref.shape
    copies = [
        pltpu.make_async_copy(q_ref, q_out, sems.at[0]),
        pltpu.make_async_copy(grad_ref, grad_out, sems.at[1]),
    ]
    for copy in copies:
        copy.start()
    sums = sums_ref[...] + other_ref[...]
    next_ref[...], slope_ref[...] = update_freqs(
        freqs_ref[...], sums[:, :width], sums[:, width:], sample_count
    )
    copies += [
        pltpu.make_async_copy(next_ref, next_out, sems.at[2]),
        pltpu.make_async_copy(slope_ref, slope_out, sems.at[3]),
    ]
    for copy in copies[2:]:
        copy.start()
    for copy in copies:
        copy.wait()


def final_kernel(place_ref, mine_ref, other_ref, out_hbm, out_ref, sems):
    anc, traits, width = out_ref.shape
    rows = pl.ds(anc * traits, anc)
    scale = jnp.sqrt(mine_ref[rows] + other_ref[rows] + 1e-06)
    pieces = sems.shape[0]
    size = anc // pieces
    copies = []
    for i in range(pieces):
        rows = pl.ds(i * size * traits, size * traits)
        total = mine_ref[rows] + other_ref[rows]
        at = pl.ds(i * size, size)
        out_ref[at] = total.reshape(size, traits, width) / scale[i * size : (i + 1) * size, None, :]
        copies.append(pltpu.make_async_copy(out_ref.at[at], out_hbm.at[at], sems.at[i]))
        copies[-1].start()
    for copy in copies:
        copy.wait()


def update_freqs(freqs, excess_sum, second_sum, sample_count):
    allele_sum = excess_sum + second_sum
    freq_next = freqs * allele_sum / (freqs * allele_sum + (1.0 - freqs) * second_sum)
    freq_gradient = excess_sum * freqs.shape[0] / math.sqrt(sample_count)
    return (freq_next, freq_gradient)


VMEM = pltpu.VMEM
SCALARS = pl.BlockSpec(memory_space=pltpu.SMEM)
IN_VMEM = pl.BlockSpec(memory_space=pltpu.VMEM)


def call(kernel, args, outs, scratch=(), cost=2000, aliases=None, raw=()):
    specs = [SCALARS]
    held = [args[0]]
    for at, x in enumerate(args[1:], 1):
        specs.append(pl.BlockSpec(memory_space=pltpu.HBM) if at in raw else IN_VMEM)
        held.append(x if at in raw else pltpu.with_memory_space_constraint(x, VMEM))
    out_specs, out_shape = [], []
    for out in outs:
        if isinstance(out, jax.ShapeDtypeStruct):
            out_specs.append(pl.BlockSpec(memory_space=pltpu.HBM))
            out_shape.append(out)
        else:
            out_specs.append(IN_VMEM)
            out_shape.append(VMEM(out, F32) if isinstance(out, tuple) else out)
    return pl.pallas_call(
        kernel,
        in_specs=specs,
        out_specs=out_specs,
        out_shape=out_shape,
        scratch_shapes=list(scratch),
        input_output_aliases=aliases or {},
        cost_estimate=pl.CostEstimate(flops=cost * 400_000, bytes_accessed=0, transcendentals=0),
        compiler_params=pltpu.CompilerParams(vmem_limit_bytes=VMEM_LIMIT),
    )(*held)


def shards(genotypes, ancestry_counts, residuals, freqs):
    var_count = lax.axis_size("var")
    rows, width = genotypes.shape
    share = rows // var_count
    half = var_count // 2
    anc = freqs.shape[0]
    traits = residuals.shape[1]
    sample_count = rows * lax.axis_size("smp")
    variants = width * var_count
    place = lax.axis_index("var").astype(jnp.int32).reshape(1)
    dma = pltpu.SemaphoreType.DMA

    def move(x, m):
        return lax.ppermute(x, "var", [(i, i ^ m) for i in range(var_count)])

    def swap(x):
        return lax.ppermute(x, "smp", [(0, 1), (1, 0)])

    half_rows = rows // 2
    pieces = 1
    excess = VMEM((half_rows, 2 * width), BF16)

    far, geno, counts = call(
        functools.partial(far_kernel, half),
        (place, genotypes, ancestry_counts.T, freqs),
        [(half, anc, share), VMEM(genotypes.shape, genotypes.dtype), VMEM((anc, rows), jnp.int32)],
        [excess, VMEM(freqs.shape, F32), dma((3, pieces + 1))],
        raw=(1, 2, 3),
    )
    (near,) = call(
        functools.partial(near_kernel, half),
        (place, geno, counts, freqs),
        [(half, anc, share)],
        [excess],
    )
    pairs = far.reshape(half // 2, 2, anc, share)
    joined = pairs[:, 0] + move(pairs[:, 1], 1)
    arrived = [near[0]] + [move(near[m], m) for m in range(1, half)]
    arrived += [move(joined[c], half + 2 * c) for c in range(half // 2)]

    halves = VMEM((rows, 2 * width), BF16)
    sums, trait_parts, count_parts = call(
        functools.partial(sums_kernel, True),
        (place, geno, counts, freqs, residuals.T),
        [(anc, 2 * width), (var_count, traits, share), (var_count, anc, share)],
        [halves],
        cost=1200,
    )
    (sums,) = call(
        functools.partial(sums_kernel, False),
        (place, geno, counts, freqs, sums),
        [(anc, 2 * width)],
        [halves],
        cost=1000,
    )
    sums_other = swap(sums)

    q_new, own_gradient = call(
        functools.partial(share_kernel, variants),
        (place, count_parts, *arrived),
        [(anc, share), (anc, share)],
        cost=500,
    )

    shares = {0: q_new}
    for m in (*range(half, var_count, 2), *range(1, half)):
        shares[m] = move(q_new, m)
    for m in range(half + 1, var_count, 2):
        shares[m] = move(shares[m - 1], 1)

    groups = (
        (0,),
        (*reversed(range(1, half - 1)), *range(half, var_count, 2)),
        (half - 1, *range(half + 1, var_count - 1, 2)),
        (var_count - 1,),
    )
    total = None
    for ms in groups:
        inputs = (geno, trait_parts, freqs) + (() if total is None else (total,))
        total, trait_parts = call(
            functools.partial(score_kernel, ms, total is None),
            (place, *[shares[m] for m in ms], *inputs),
            [((anc * traits + anc), width), trait_parts.shape],
            cost=700 * len(ms),
            aliases={len(ms) + 2: 1} | ({} if total is None else {len(ms) + 4: 0}),
        )
    total_other = swap(total)
    out = jax.ShapeDtypeStruct
    q_out, grad_out, freq_next, freq_gradient = call(
        functools.partial(emit_kernel, sample_count),
        (place, q_new, own_gradient, sums, sums_other, freqs),
        [out((anc, share), F32)] * 2 + [out((anc, width), F32)] * 2,
        [VMEM((anc, width), F32)] * 2 + [dma((4,))],
        cost=600,
    )
    (z_score,) = call(
        final_kernel,
        (place, total, total_other),
        [out((anc, traits, width), F32)],
        [VMEM((anc, traits, width), F32), dma((4 if anc % 4 == 0 else 1,))],
        cost=300,
    )
    return (q_out.T, grad_out.T, freq_next, freq_gradient, z_score)


def plain_shards(genotypes, ancestry_counts, residuals, freqs):
    highest = lax.Precision.HIGHEST
    var_count = lax.axis_size("var")
    rows, width = genotypes.shape
    share = rows // var_count
    anc = freqs.shape[0]
    traits = residuals.shape[1]
    counts = ancestry_counts.astype(F32)
    fractions = counts / jnp.sum(counts, axis=1, keepdims=True)
    dosage = genotypes.astype(F32)
    recon = jnp.dot(fractions, freqs, precision=highest)
    ratio_a = dosage / recon
    ratio_b = (2.0 - dosage) / (1.0 - recon)
    excess = ratio_a - ratio_b
    gradient, second = lax.psum(
        (jnp.dot(excess, freqs.T, precision=highest), jnp.sum(ratio_b, axis=1)), "var"
    )
    excess_sum, second_sum = lax.psum(
        (
            jnp.dot(fractions.T, excess, precision=highest),
            jnp.dot(fractions.T, ratio_b, precision=highest),
        ),
        "smp",
    )
    freq_next, freq_gradient = update_freqs(
        freqs, excess_sum, second_sum, rows * lax.axis_size("smp")
    )
    weighted = fractions * (gradient + second[:, None])
    q_new = weighted / jnp.sum(weighted, axis=1, keepdims=True)
    first_row = lax.axis_index("var") * share
    own_next = lax.dynamic_slice_in_dim(q_new, first_row, share, 0)
    own_gradient = lax.dynamic_slice_in_dim(gradient, first_row, share, 0)
    ratio = dosage / jnp.dot(q_new, freqs, precision=highest)
    residual = residuals.astype(F32) / 1000.0
    products = (q_new[:, :, None] * residual[:, None, :]).reshape(rows, anc * traits)
    score, info = lax.psum(
        (
            jnp.dot(products.T, ratio, precision=highest),
            jnp.dot((q_new * q_new).T, ratio * ratio, precision=highest),
        ),
        "smp",
    )
    tiles = score.reshape(anc, traits, width)
    z_score = tiles / jnp.sqrt(info + 1e-06)[:, None, :]
    return (own_next, own_gradient / math.sqrt(width * var_count), freq_next, freq_gradient, z_score)


def solution(mesh):
    sizes = dict(mesh.shape)

    def step(genotypes, ancestry_counts, residuals, freqs):
        rows = genotypes.shape[0] // (sizes["grp"] * sizes["smp"])
        power = sizes["var"] & (sizes["var"] - 1) == 0 and sizes["var"] >= 4
        tiled = rows % (16 * sizes["var"]) == 0 and rows % (2 * LANES) == 0
        in_specs = (
            P(("grp", "smp"), "var"),
            P(("grp", "smp"), None),
            P(("grp", "smp"), None),
            P("grp", "var"),
        )
        out_specs = (
            P(("grp", "smp", "var"), None),
            P(("grp", "smp", "var"), None),
            P("grp", "var"),
            P("grp", "var"),
            P("grp", None, "var"),
        )
        fits = power and tiled and sizes["smp"] == 2

        def body(*args):
            return (shards if fits else plain_shards)(*args)

        mapped = jax.shard_map(
            body,
            mesh=mesh,
            in_specs=in_specs,
            out_specs=out_specs,
            check_vma=False,
        )
        return mapped(genotypes, ancestry_counts, residuals, freqs)

    return step
```

```python
import functools
import math

import jax
import jax.numpy as jnp
from jax import lax
from jax.experimental import pallas as pl
from jax.experimental.pallas import tpu as pltpu
from jax.sharding import PartitionSpec as P


F32 = jnp.float32
BF16 = jnp.bfloat16
LANES = 128
VMEM_LIMIT = 60 * 1024 * 1024
NN = ((1,), (0,))
NT = ((1,), (1,))
TN = ((0,), (0,))


def split(x):
    high = x.astype(BF16)
    return high, (x - high.astype(F32)).astype(BF16)


def dot(a, b, dims):
    return lax.dot_general(a, b, (dims, ((), ())), preferred_element_type=F32)


def count_table(freqs):
    high, middle = split(freqs)
    low = (freqs - high.astype(F32) - middle.astype(F32)).astype(BF16)
    ones = jnp.ones_like(high)
    zeros = jnp.zeros_like(high)
    left = jnp.concatenate([high, middle, low], axis=0)
    return jnp.concatenate([left, jnp.concatenate([ones, zeros, zeros], axis=0)], axis=1)


def ratio_parts(counts, dosage, table):
    width = dosage.shape[1]
    both = dot(jnp.concatenate([counts, counts, counts], axis=0), table, TN)
    recon, total = both[:, :width], both[:, width:]
    inverse = 1.0 / (recon * (total - recon))
    part = (dosage * total - (recon + recon)) * inverse
    return part, recon, inverse, total


def half_gradient(shares, place, start, geno_ref, counts_ref, freqs, grad_ref, excess_ref, before):
    half_rows = excess_ref.shape[0]
    anc, width = freqs.shape
    table = count_table(freqs)
    for row in range(0, half_rows, LANES):
        before(row)
        first = pl.multiple_of(start + row, LANES)
        counts = counts_ref[:, pl.ds(first, LANES)].astype(F32).astype(BF16)
        dosage = geno_ref[pl.ds(first, LANES), :].astype(F32)
        part, _, _, total = ratio_parts(counts, dosage, table)
        high, low = split(part * total)
        excess_ref[pl.ds(row, LANES), :width] = high
        excess_ref[pl.ds(row, LANES), width:] = low
    left = jnp.concatenate(split(freqs), axis=0)
    grads = dot(jnp.concatenate([left, left], axis=1), excess_ref[...], NT)
    grads = grads[:anc] + grads[anc:]
    share = half_rows // shares
    for c in range(shares):
        grad_ref[c ^ (place % shares)] = grads[:, c * share : (c + 1) * share]


def far_kernel(
    shares, place_ref, geno_hbm, counts_hbm, freqs_hbm, grad_ref, geno_ref, counts_ref, excess_ref, freqs_ref, sems
):
    half_rows = excess_ref.shape[0]
    pieces = sems.shape[1] - 1
    size = half_rows // pieces
    place = place_ref[0]
    own_half = place // shares
    far = (1 - own_half) * half_rows
    near = own_half * half_rows

    def pair(first, count, at):
        rows = pl.ds(pl.multiple_of(first, LANES), count)
        return (
            pltpu.make_async_copy(counts_hbm.at[:, rows], counts_ref.at[:, rows], sems.at[0, at]),
            pltpu.make_async_copy(geno_hbm.at[rows, :], geno_ref.at[rows, :], sems.at[1, at]),
        )

    freqs_copy = pltpu.make_async_copy(freqs_hbm, freqs_ref, sems.at[2, 0])
    freqs_copy.start()
    moves = [pair(far + i * size, size, i) for i in range(pieces)]
    moves.append(pair(near, half_rows, pieces))
    for move in moves[:pieces]:
        for copy in move:
            copy.start()
    freqs_copy.wait()

    def before(row):
        if row % size == 0:
            for copy in moves[row // size]:
                copy.wait()
        if row == half_rows // 2 // size * size:
            for copy in moves[pieces]:
                copy.start()

    half_gradient(shares, place, far, geno_ref, counts_ref, freqs_ref[...], grad_ref, excess_ref, before)
    for copy in moves[pieces]:
        copy.wait()


def near_kernel(shares, place_ref, geno_ref, counts_ref, freqs_ref, grad_ref, excess_ref):
    place = place_ref[0]
    start = (place // shares) * excess_ref.shape[0]
    half_gradient(
        shares, place, start, geno_ref, counts_ref, freqs_ref[...], grad_ref, excess_ref, lambda row: None
    )


def sums_kernel(first, place_ref, geno_ref, counts_ref, freqs_ref, *refs):
    other_ref, refs = refs[0], refs[1:]
    sums_ref, parts_ref = refs[0], refs[-1]
    half_rows = parts_ref.shape[0] // 2
    width = freqs_ref.shape[1]
    start = 0 if first else half_rows
    table = count_table(freqs_ref[...])
    for row in range(0, half_rows, LANES):
        counts = counts_ref[:, pl.ds(start + row, LANES)].astype(F32).astype(BF16)
        dosage = geno_ref[pl.ds(start + row, LANES), :].astype(F32)
        part, recon, inverse, _ = ratio_parts(counts, dosage, table)
        for at, value in enumerate((part, (2.0 - dosage) * (recon * inverse))):
            high, low = split(value)
            parts_ref[pl.ds(row, LANES), pl.ds(at * width, width)] = high
            parts_ref[pl.ds(half_rows + row, LANES), pl.ds(at * width, width)] = low
    left = counts_ref[:, pl.ds(start, half_rows)].astype(F32).astype(BF16)
    sums = dot(jnp.concatenate([left, left], axis=1), parts_ref[...], NN)
    if not first:
        sums_ref[...] = sums + other_ref[...]
        return
    sums_ref[...] = sums
    traits_ref, own_ref = refs[1:3]
    residual = other_ref[...].astype(F32) / 1000.0
    counts = counts_ref[...].astype(F32)
    share = traits_ref.shape[2]
    for c in range(traits_ref.shape[0]):
        traits_ref[c] = residual[:, c * share : (c + 1) * share]
        own_ref[c] = counts[:, c * share : (c + 1) * share]


def share_kernel(variants, own_ref, counts_ref, *refs):
    q_ref, grad_ref = refs[-2:]
    gradient = sum(part[...] for part in refs[1:-2]) + refs[0][...]
    counts = counts_ref[own_ref[0]]
    fractions = counts / jnp.sum(counts, axis=0, keepdims=True)
    second = 2.0 * variants - jnp.sum(fractions * gradient, axis=0, keepdims=True)
    weighted = fractions * (gradient + second)
    q_ref[...] = weighted / jnp.sum(weighted, axis=0, keepdims=True)
    grad_ref[...] = gradient / math.sqrt(variants)


def score_kernel(shares, fresh, own_ref, *refs):
    q_refs, refs = refs[: len(shares)], refs[len(shares) :]
    geno_ref, traits_ref, freqs_ref = refs[:3]
    out_ref = refs[-2]
    freq_high, freq_low = split(freqs_ref[...])
    f_three = jnp.concatenate([freq_high, freq_high, freq_low], axis=0)
    anc, width = freqs_ref.shape
    traits = traits_ref.shape[1]
    for m, q_ref in zip(shares, q_refs):
        q_new = q_ref[...]
        rows = q_new.shape[1]
        owner = own_ref[0] ^ m
        q_high, q_low = split(q_new)
        recon = dot(jnp.concatenate([q_high, q_low, q_high], axis=0), f_three, TN)
        dosage = geno_ref[pl.ds(pl.multiple_of(owner * rows, 16), rows), :].astype(F32)
        ratio = dosage / recon
        ratio_high, ratio_low = split(ratio)
        right = jnp.concatenate([ratio_high, ratio_low], axis=1)
        square_high, square_low = split(ratio * ratio)
        q2_high, q2_low = split(q_new * q_new)
        residual = traits_ref[owner]
        products = (q_new[:, None, :] * residual[None, :, :]).reshape(anc * traits, rows)
        high, low = split(products)
        wide = dot(high, right, NN)
        part = wide[:, :width] + wide[:, width:] + dot(low, ratio_high, NN)
        wide2 = dot(
            jnp.concatenate([q2_high, q2_low], axis=0),
            jnp.concatenate([square_high, square_low], axis=1),
            NN,
        )
        part2 = wide2[:anc, :width] + wide2[:anc, width:] + wide2[anc:, :width]
        if fresh and m == shares[0]:
            out_ref[: anc * traits] = part
            out_ref[anc * traits :] = part2
        else:
            out_ref[: anc * traits] += part
            out_ref[anc * traits :] += part2


def emit_kernel(
    sample_count, place_ref, q_ref, grad_ref, sums_ref, other_ref, freqs_ref, q_out, grad_out, next_out, slope_out, next_ref, slope_ref, sems
):
    _, width = freqs_ref.shape
    copies = [
        pltpu.make_async_copy(q_ref, q_out, sems.at[0]),
        pltpu.make_async_copy(grad_ref, grad_out, sems.at[1]),
    ]
    for copy in copies:
        copy.start()
    sums = sums_ref[...] + other_ref[...]
    next_ref[...], slope_ref[...] = update_freqs(
        freqs_ref[...], sums[:, :width], sums[:, width:], sample_count
    )
    copies += [
        pltpu.make_async_copy(next_ref, next_out, sems.at[2]),
        pltpu.make_async_copy(slope_ref, slope_out, sems.at[3]),
    ]
    for copy in copies[2:]:
        copy.start()
    for copy in copies:
        copy.wait()


def final_kernel(place_ref, mine_ref, other_ref, out_hbm, out_ref, sems):
    anc, traits, width = out_ref.shape
    rows = pl.ds(anc * traits, anc)
    scale = jnp.sqrt(mine_ref[rows] + other_ref[rows] + 1e-06)
    pieces = sems.shape[0]
    size = anc // pieces
    copies = []
    for i in range(pieces):
        rows = pl.ds(i * size * traits, size * traits)
        total = mine_ref[rows] + other_ref[rows]
        at = pl.ds(i * size, size)
        out_ref[at] = total.reshape(size, traits, width) / scale[i * size : (i + 1) * size, None, :]
        copies.append(pltpu.make_async_copy(out_ref.at[at], out_hbm.at[at], sems.at[i]))
        copies[-1].start()
    for copy in copies:
        copy.wait()


def update_freqs(freqs, excess_sum, second_sum, sample_count):
    allele_sum = excess_sum + second_sum
    freq_next = freqs * allele_sum / (freqs * allele_sum + (1.0 - freqs) * second_sum)
    freq_gradient = excess_sum * freqs.shape[0] / math.sqrt(sample_count)
    return (freq_next, freq_gradient)


VMEM = pltpu.VMEM
SCALARS = pl.BlockSpec(memory_space=pltpu.SMEM)
IN_VMEM = pl.BlockSpec(memory_space=pltpu.VMEM)


def call(kernel, args, outs, scratch=(), cost=2000, aliases=None, raw=()):
    specs = [SCALARS]
    held = [args[0]]
    for at, x in enumerate(args[1:], 1):
        specs.append(pl.BlockSpec(memory_space=pltpu.HBM) if at in raw else IN_VMEM)
        held.append(x if at in raw else pltpu.with_memory_space_constraint(x, VMEM))
    out_specs, out_shape = [], []
    for out in outs:
        if isinstance(out, jax.ShapeDtypeStruct):
            out_specs.append(pl.BlockSpec(memory_space=pltpu.HBM))
            out_shape.append(out)
        else:
            out_specs.append(IN_VMEM)
            out_shape.append(VMEM(out, F32) if isinstance(out, tuple) else out)
    return pl.pallas_call(
        kernel,
        in_specs=specs,
        out_specs=out_specs,
        out_shape=out_shape,
        scratch_shapes=list(scratch),
        input_output_aliases=aliases or {},
        cost_estimate=pl.CostEstimate(flops=cost * 400_000, bytes_accessed=0, transcendentals=0),
        compiler_params=pltpu.CompilerParams(vmem_limit_bytes=VMEM_LIMIT),
    )(*held)


def shards(genotypes, ancestry_counts, residuals, freqs):
    var_count = lax.axis_size("var")
    rows, width = genotypes.shape
    share = rows // var_count
    half = var_count // 2
    anc = freqs.shape[0]
    traits = residuals.shape[1]
    sample_count = rows * lax.axis_size("smp")
    variants = width * var_count
    place = lax.axis_index("var").astype(jnp.int32).reshape(1)
    dma = pltpu.SemaphoreType.DMA

    def move(x, m):
        return lax.ppermute(x, "var", [(i, i ^ m) for i in range(var_count)])

    def swap(x):
        return lax.ppermute(x, "smp", [(0, 1), (1, 0)])

    half_rows = rows // 2
    pieces = 1
    excess = VMEM((half_rows, 2 * width), BF16)

    far, geno, counts = call(
        functools.partial(far_kernel, half),
        (place, genotypes, ancestry_counts.T, freqs),
        [(half, anc, share), VMEM(genotypes.shape, genotypes.dtype), VMEM((anc, rows), jnp.int32)],
        [excess, VMEM(freqs.shape, F32), dma((3, pieces + 1))],
        raw=(1, 2, 3),
    )
    (near,) = call(
        functools.partial(near_kernel, half),
        (place, geno, counts, freqs),
        [(half, anc, share)],
        [excess],
    )
    pairs = far.reshape(half // 2, 2, anc, share)
    joined = pairs[:, 0] + move(pairs[:, 1], 1)
    arrived = [near[0]] + [move(near[m], m) for m in range(1, half)]
    arrived += [move(joined[c], half + 2 * c) for c in range(half // 2)]

    halves = VMEM((rows, 2 * width), BF16)
    sums, trait_parts, count_parts = call(
        functools.partial(sums_kernel, True),
        (place, geno, counts, freqs, residuals.T),
        [(anc, 2 * width), (var_count, traits, share), (var_count, anc, share)],
        [halves],
        cost=1200,
    )
    (sums,) = call(
        functools.partial(sums_kernel, False),
        (place, geno, counts, freqs, sums),
        [(anc, 2 * width)],
        [halves],
        cost=1000,
    )
    sums_other = swap(sums)

    q_new, own_gradient = call(
        functools.partial(share_kernel, variants),
        (place, count_parts, *arrived),
        [(anc, share), (anc, share)],
        cost=500,
    )

    shares = {0: q_new}
    for m in (*range(half, var_count, 2), *range(1, half)):
        shares[m] = move(q_new, m)
    for m in range(half + 1, var_count, 2):
        shares[m] = move(shares[m - 1], 1)

    groups = (
        (0,),
        (*reversed(range(1, half - 1)), *range(half, var_count, 2)),
        (half - 1, *range(half + 1, var_count - 1, 2)),
        (var_count - 1,),
    )
    total = None
    for ms in groups:
        inputs = (geno, trait_parts, freqs) + (() if total is None else (total,))
        total, trait_parts = call(
            functools.partial(score_kernel, ms, total is None),
            (place, *[shares[m] for m in ms], *inputs),
            [((anc * traits + anc), width), trait_parts.shape],
            cost=700 * len(ms),
            aliases={len(ms) + 2: 1} | ({} if total is None else {len(ms) + 4: 0}),
        )
    total_other = swap(total)
    out = jax.ShapeDtypeStruct
    q_out, grad_out, freq_next, freq_gradient = call(
        functools.partial(emit_kernel, sample_count),
        (place, q_new, own_gradient, sums, sums_other, freqs),
        [out((anc, share), F32)] * 2 + [out((anc, width), F32)] * 2,
        [VMEM((anc, width), F32)] * 2 + [dma((4,))],
        cost=600,
    )
    (z_score,) = call(
        final_kernel,
        (place, total, total_other),
        [out((anc, traits, width), F32)],
        [VMEM((anc, traits, width), F32), dma((4 if anc % 4 == 0 else 1,))],
        cost=300,
    )
    return (q_out.T, grad_out.T, freq_next, freq_gradient, z_score)


def plain_shards(genotypes, ancestry_counts, residuals, freqs):
    highest = lax.Precision.HIGHEST
    var_count = lax.axis_size("var")
    rows, width = genotypes.shape
    share = rows // var_count
    anc = freqs.shape[0]
    traits = residuals.shape[1]
    counts = ancestry_counts.astype(F32)
    fractions = counts / jnp.sum(counts, axis=1, keepdims=True)
    dosage = genotypes.astype(F32)
    recon = jnp.dot(fractions, freqs, precision=highest)
    ratio_a = dosage / recon
    ratio_b = (2.0 - dosage) / (1.0 - recon)
    excess = ratio_a - ratio_b
    gradient, second = lax.psum(
        (jnp.dot(excess, freqs.T, precision=highest), jnp.sum(ratio_b, axis=1)), "var"
    )
    excess_sum, second_sum = lax.psum(
        (
            jnp.dot(fractions.T, excess, precision=highest),
            jnp.dot(fractions.T, ratio_b, precision=highest),
        ),
        "smp",
    )
    freq_next, freq_gradient = update_freqs(
        freqs, excess_sum, second_sum, rows * lax.axis_size("smp")
    )
    weighted = fractions * (gradient + second[:, None])
    q_new = weighted / jnp.sum(weighted, axis=1, keepdims=True)
    first_row = lax.axis_index("var") * share
    own_next = lax.dynamic_slice_in_dim(q_new, first_row, share, 0)
    own_gradient = lax.dynamic_slice_in_dim(gradient, first_row, share, 0)
    ratio = dosage / jnp.dot(q_new, freqs, precision=highest)
    residual = residuals.astype(F32) / 1000.0
    products = (q_new[:, :, None] * residual[:, None, :]).reshape(rows, anc * traits)
    score, info = lax.psum(
        (
            jnp.dot(products.T, ratio, precision=highest),
            jnp.dot((q_new * q_new).T, ratio * ratio, precision=highest),
        ),
        "smp",
    )
    tiles = score.reshape(anc, traits, width)
    z_score = tiles / jnp.sqrt(info + 1e-06)[:, None, :]
    return (own_next, own_gradient / math.sqrt(width * var_count), freq_next, freq_gradient, z_score)


def solution(mesh):
    sizes = dict(mesh.shape)

    def step(genotypes, ancestry_counts, residuals, freqs):
        rows = genotypes.shape[0] // (sizes["grp"] * sizes["smp"])
        power = sizes["var"] & (sizes["var"] - 1) == 0 and sizes["var"] >= 4
        tiled = rows % (16 * sizes["var"]) == 0 and rows % (2 * LANES) == 0
        in_specs = (
            P(("grp", "smp"), "var"),
            P(("grp", "smp"), None),
            P(("grp", "smp"), None),
            P("grp", "var"),
        )
        out_specs = (
            P(("grp", "smp", "var"), None),
            P(("grp", "smp", "var"), None),
            P("grp", "var"),
            P("grp", "var"),
            P("grp", None, "var"),
        )
        fits = power and tiled and sizes["smp"] == 2

        def body(*args):
            return (shards if fits else plain_shards)(*args)

        mapped = jax.shard_map(
            body,
            mesh=mesh,
            in_specs=in_specs,
            out_specs=out_specs,
            check_vma=False,
        )
        return mapped(genotypes, ancestry_counts, residuals, freqs)

    return step
```

```python
import functools
import math

import jax
import jax.numpy as jnp
from jax import lax
from jax.experimental import pallas as pl
from jax.experimental.pallas import tpu as pltpu
from jax.sharding import PartitionSpec as P


F32 = jnp.float32
BF16 = jnp.bfloat16
LANES = 128
VMEM_LIMIT = 60 * 1024 * 1024
NN = ((1,), (0,))
NT = ((1,), (1,))
TN = ((0,), (0,))


def split(x):
    high = x.astype(BF16)
    return high, (x - high.astype(F32)).astype(BF16)


def dot(a, b, dims):
    return lax.dot_general(a, b, (dims, ((), ())), preferred_element_type=F32)


def count_table(freqs):
    high, middle = split(freqs)
    low = (freqs - high.astype(F32) - middle.astype(F32)).astype(BF16)
    ones = jnp.ones_like(high)
    zeros = jnp.zeros_like(high)
    left = jnp.concatenate([high, middle, low], axis=0)
    return jnp.concatenate([left, jnp.concatenate([ones, zeros, zeros], axis=0)], axis=1)


def ratio_parts(counts, dosage, table):
    width = dosage.shape[1]
    both = dot(jnp.concatenate([counts, counts, counts], axis=0), table, TN)
    recon, total = both[:, :width], both[:, width:]
    inverse = 1.0 / (recon * (total - recon))
    part = (dosage * total - (recon + recon)) * inverse
    return part, recon, inverse, total


def half_gradient(shares, place, start, geno_ref, counts_ref, freqs, grad_ref, excess_ref, before):
    half_rows = excess_ref.shape[0]
    anc, width = freqs.shape
    table = count_table(freqs)
    for row in range(0, half_rows, LANES):
        before(row)
        first = pl.multiple_of(start + row, LANES)
        counts = counts_ref[:, pl.ds(first, LANES)].astype(F32).astype(BF16)
        dosage = geno_ref[pl.ds(first, LANES), :].astype(F32)
        part, _, _, total = ratio_parts(counts, dosage, table)
        high, low = split(part * total)
        excess_ref[pl.ds(row, LANES), :width] = high
        excess_ref[pl.ds(row, LANES), width:] = low
    left = jnp.concatenate(split(freqs), axis=0)
    grads = dot(jnp.concatenate([left, left], axis=1), excess_ref[...], NT)
    grads = grads[:anc] + grads[anc:]
    share = half_rows // shares
    for c in range(shares):
        grad_ref[c ^ (place % shares)] = grads[:, c * share : (c + 1) * share]


def far_kernel(
    shares, place_ref, geno_hbm, counts_hbm, freqs_hbm, grad_ref, geno_ref, counts_ref, excess_ref, freqs_ref, sems
):
    half_rows = excess_ref.shape[0]
    pieces = sems.shape[1] - 1
    size = half_rows // pieces
    place = place_ref[0]
    own_half = place // shares
    far = (1 - own_half) * half_rows
    near = own_half * half_rows

    def pair(first, count, at):
        rows = pl.ds(pl.multiple_of(first, LANES), count)
        return (
            pltpu.make_async_copy(counts_hbm.at[:, rows], counts_ref.at[:, rows], sems.at[0, at]),
            pltpu.make_async_copy(geno_hbm.at[rows, :], geno_ref.at[rows, :], sems.at[1, at]),
        )

    freqs_copy = pltpu.make_async_copy(freqs_hbm, freqs_ref, sems.at[2, 0])
    freqs_copy.start()
    moves = [pair(far + i * size, size, i) for i in range(pieces)]
    moves.append(pair(near, half_rows, pieces))
    for move in moves[:pieces]:
        for copy in move:
            copy.start()
    freqs_copy.wait()

    def before(row):
        if row % size == 0:
            for copy in moves[row // size]:
                copy.wait()
        if row == half_rows // 2 // size * size:
            for copy in moves[pieces]:
                copy.start()

    half_gradient(shares, place, far, geno_ref, counts_ref, freqs_ref[...], grad_ref, excess_ref, before)
    for copy in moves[pieces]:
        copy.wait()


def near_kernel(shares, place_ref, geno_ref, counts_ref, freqs_ref, grad_ref, excess_ref):
    place = place_ref[0]
    start = (place // shares) * excess_ref.shape[0]
    half_gradient(
        shares, place, start, geno_ref, counts_ref, freqs_ref[...], grad_ref, excess_ref, lambda row: None
    )


def sums_kernel(first, place_ref, geno_ref, counts_ref, freqs_ref, *refs):
    other_ref, refs = refs[0], refs[1:]
    sums_ref, parts_ref = refs[0], refs[-1]
    half_rows = parts_ref.shape[0] // 2
    width = freqs_ref.shape[1]
    start = 0 if first else half_rows
    table = count_table(freqs_ref[...])
    for row in range(0, half_rows, LANES):
        counts = counts_ref[:, pl.ds(start + row, LANES)].astype(F32).astype(BF16)
        dosage = geno_ref[pl.ds(start + row, LANES), :].astype(F32)
        part, recon, inverse, _ = ratio_parts(counts, dosage, table)
        for at, value in enumerate((part, (2.0 - dosage) * (recon * inverse))):
            high, low = split(value)
            parts_ref[pl.ds(row, LANES), pl.ds(at * width, width)] = high
            parts_ref[pl.ds(half_rows + row, LANES), pl.ds(at * width, width)] = low
    left = counts_ref[:, pl.ds(start, half_rows)].astype(F32).astype(BF16)
    sums = dot(jnp.concatenate([left, left], axis=1), parts_ref[...], NN)
    if not first:
        sums_ref[...] = sums + other_ref[...]
        return
    sums_ref[...] = sums
    traits_ref, own_ref = refs[1:3]
    residual = other_ref[...].astype(F32) / 1000.0
    counts = counts_ref[...].astype(F32)
    share = traits_ref.shape[2]
    for c in range(traits_ref.shape[0]):
        traits_ref[c] = residual[:, c * share : (c + 1) * share]
        own_ref[c] = counts[:, c * share : (c + 1) * share]


def share_kernel(variants, own_ref, counts_ref, *refs):
    q_ref, grad_ref = refs[-2:]
    gradient = sum(part[...] for part in refs[1:-2]) + refs[0][...]
    counts = counts_ref[own_ref[0]]
    fractions = counts / jnp.sum(counts, axis=0, keepdims=True)
    second = 2.0 * variants - jnp.sum(fractions * gradient, axis=0, keepdims=True)
    weighted = fractions * (gradient + second)
    q_ref[...] = weighted / jnp.sum(weighted, axis=0, keepdims=True)
    grad_ref[...] = gradient / math.sqrt(variants)


def score_kernel(shares, fresh, own_ref, *refs):
    q_refs, refs = refs[: len(shares)], refs[len(shares) :]
    geno_ref, traits_ref, freqs_ref = refs[:3]
    out_ref = refs[-2]
    freq_high, freq_low = split(freqs_ref[...])
    f_three = jnp.concatenate([freq_high, freq_high, freq_low], axis=0)
    anc, width = freqs_ref.shape
    traits = traits_ref.shape[1]
    for m, q_ref in zip(shares, q_refs):
        q_new = q_ref[...]
        rows = q_new.shape[1]
        owner = own_ref[0] ^ m
        q_high, q_low = split(q_new)
        recon = dot(jnp.concatenate([q_high, q_low, q_high], axis=0), f_three, TN)
        dosage = geno_ref[pl.ds(pl.multiple_of(owner * rows, 16), rows), :].astype(F32)
        ratio = dosage / recon
        ratio_high, ratio_low = split(ratio)
        right = jnp.concatenate([ratio_high, ratio_low], axis=1)
        square_high, square_low = split(ratio * ratio)
        q2_high, q2_low = split(q_new * q_new)
        residual = traits_ref[owner]
        products = (q_new[:, None, :] * residual[None, :, :]).reshape(anc * traits, rows)
        high, low = split(products)
        wide = dot(high, right, NN)
        part = wide[:, :width] + wide[:, width:] + dot(low, ratio_high, NN)
        wide2 = dot(
            jnp.concatenate([q2_high, q2_low], axis=0),
            jnp.concatenate([square_high, square_low], axis=1),
            NN,
        )
        part2 = wide2[:anc, :width] + wide2[:anc, width:] + wide2[anc:, :width]
        if fresh and m == shares[0]:
            out_ref[: anc * traits] = part
            out_ref[anc * traits :] = part2
        else:
            out_ref[: anc * traits] += part
            out_ref[anc * traits :] += part2


def emit_kernel(
    sample_count, place_ref, q_ref, grad_ref, sums_ref, other_ref, freqs_ref, q_out, grad_out, next_out, slope_out, next_ref, slope_ref, sems
):
    _, width = freqs_ref.shape
    copies = [
        pltpu.make_async_copy(q_ref, q_out, sems.at[0]),
        pltpu.make_async_copy(grad_ref, grad_out, sems.at[1]),
    ]
    for copy in copies:
        copy.start()
    sums = sums_ref[...] + other_ref[...]
    next_ref[...], slope_ref[...] = update_freqs(
        freqs_ref[...], sums[:, :width], sums[:, width:], sample_count
    )
    copies += [
        pltpu.make_async_copy(next_ref, next_out, sems.at[2]),
        pltpu.make_async_copy(slope_ref, slope_out, sems.at[3]),
    ]
    for copy in copies[2:]:
        copy.start()
    for copy in copies:
        copy.wait()


def final_kernel(place_ref, mine_ref, other_ref, out_hbm, out_ref, sems):
    anc, traits, width = out_ref.shape
    rows = pl.ds(anc * traits, anc)
    scale = jnp.sqrt(mine_ref[rows] + other_ref[rows] + 1e-06)
    pieces = sems.shape[0]
    size = anc // pieces
    copies = []
    for i in range(pieces):
        rows = pl.ds(i * size * traits, size * traits)
        total = mine_ref[rows] + other_ref[rows]
        at = pl.ds(i * size, size)
        out_ref[at] = total.reshape(size, traits, width) / scale[i * size : (i + 1) * size, None, :]
        copies.append(pltpu.make_async_copy(out_ref.at[at], out_hbm.at[at], sems.at[i]))
        copies[-1].start()
    for copy in copies:
        copy.wait()


def update_freqs(freqs, excess_sum, second_sum, sample_count):
    allele_sum = excess_sum + second_sum
    freq_next = freqs * allele_sum / (freqs * allele_sum + (1.0 - freqs) * second_sum)
    freq_gradient = excess_sum * freqs.shape[0] / math.sqrt(sample_count)
    return (freq_next, freq_gradient)


VMEM = pltpu.VMEM
SCALARS = pl.BlockSpec(memory_space=pltpu.SMEM)
IN_VMEM = pl.BlockSpec(memory_space=pltpu.VMEM)


def call(kernel, args, outs, scratch=(), cost=2000, aliases=None, raw=()):
    specs = [SCALARS]
    held = [args[0]]
    for at, x in enumerate(args[1:], 1):
        specs.append(pl.BlockSpec(memory_space=pltpu.HBM) if at in raw else IN_VMEM)
        held.append(x if at in raw else pltpu.with_memory_space_constraint(x, VMEM))
    out_specs, out_shape = [], []
    for out in outs:
        if isinstance(out, jax.ShapeDtypeStruct):
            out_specs.append(pl.BlockSpec(memory_space=pltpu.HBM))
            out_shape.append(out)
        else:
            out_specs.append(IN_VMEM)
            out_shape.append(VMEM(out, F32) if isinstance(out, tuple) else out)
    return pl.pallas_call(
        kernel,
        in_specs=specs,
        out_specs=out_specs,
        out_shape=out_shape,
        scratch_shapes=list(scratch),
        input_output_aliases=aliases or {},
        cost_estimate=pl.CostEstimate(flops=cost * 400_000, bytes_accessed=0, transcendentals=0),
        compiler_params=pltpu.CompilerParams(vmem_limit_bytes=VMEM_LIMIT),
    )(*held)


def shards(genotypes, ancestry_counts, residuals, freqs):
    var_count = lax.axis_size("var")
    rows, width = genotypes.shape
    share = rows // var_count
    half = var_count // 2
    anc = freqs.shape[0]
    traits = residuals.shape[1]
    sample_count = rows * lax.axis_size("smp")
    variants = width * var_count
    place = lax.axis_index("var").astype(jnp.int32).reshape(1)
    dma = pltpu.SemaphoreType.DMA

    def move(x, m):
        return lax.ppermute(x, "var", [(i, i ^ m) for i in range(var_count)])

    def swap(x):
        return lax.ppermute(x, "smp", [(0, 1), (1, 0)])

    half_rows = rows // 2
    pieces = 1
    excess = VMEM((half_rows, 2 * width), BF16)

    far, geno, counts = call(
        functools.partial(far_kernel, half),
        (place, genotypes, ancestry_counts.T, freqs),
        [(half, anc, share), VMEM(genotypes.shape, genotypes.dtype), VMEM((anc, rows), jnp.int32)],
        [excess, VMEM(freqs.shape, F32), dma((3, pieces + 1))],
        raw=(1, 2, 3),
    )
    (near,) = call(
        functools.partial(near_kernel, half),
        (place, geno, counts, freqs),
        [(half, anc, share)],
        [excess],
    )
    pairs = far.reshape(half // 2, 2, anc, share)
    joined = pairs[:, 0] + move(pairs[:, 1], 1)
    arrived = [near[0]] + [move(near[m], m) for m in range(1, half)]
    arrived += [move(joined[c], half + 2 * c) for c in range(half // 2)]

    halves = VMEM((rows, 2 * width), BF16)
    sums, trait_parts, count_parts = call(
        functools.partial(sums_kernel, True),
        (place, geno, counts, freqs, residuals.T),
        [(anc, 2 * width), (var_count, traits, share), (var_count, anc, share)],
        [halves],
        cost=1200,
    )
    (sums,) = call(
        functools.partial(sums_kernel, False),
        (place, geno, counts, freqs, sums),
        [(anc, 2 * width)],
        [halves],
        cost=1000,
    )
    sums_other = swap(sums)

    q_new, own_gradient = call(
        functools.partial(share_kernel, variants),
        (place, count_parts, *arrived),
        [(anc, share), (anc, share)],
        cost=500,
    )

    shares = {0: q_new}
    for m in (*range(half, var_count, 2), *range(1, half)):
        shares[m] = move(q_new, m)
    for m in range(half + 1, var_count, 2):
        shares[m] = move(shares[m - 1], 1)

    groups = (
        (0,),
        (*reversed(range(1, half - 1)), half),
        (*range(half + 2, var_count, 2), half - 1, *range(half + 1, var_count - 1, 2)),
        (var_count - 1,),
    )
    total = None
    for ms in groups:
        inputs = (geno, trait_parts, freqs) + (() if total is None else (total,))
        total, trait_parts = call(
            functools.partial(score_kernel, ms, total is None),
            (place, *[shares[m] for m in ms], *inputs),
            [((anc * traits + anc), width), trait_parts.shape],
            cost=700 * len(ms),
            aliases={len(ms) + 2: 1} | ({} if total is None else {len(ms) + 4: 0}),
        )
    total_other = swap(total)
    out = jax.ShapeDtypeStruct
    q_out, grad_out, freq_next, freq_gradient = call(
        functools.partial(emit_kernel, sample_count),
        (place, q_new, own_gradient, sums, sums_other, freqs),
        [out((anc, share), F32)] * 2 + [out((anc, width), F32)] * 2,
        [VMEM((anc, width), F32)] * 2 + [dma((4,))],
        cost=600,
    )
    (z_score,) = call(
        final_kernel,
        (place, total, total_other),
        [out((anc, traits, width), F32)],
        [VMEM((anc, traits, width), F32), dma((2 if anc % 2 == 0 else 1,))],
        cost=300,
    )
    return (q_out.T, grad_out.T, freq_next, freq_gradient, z_score)


def plain_shards(genotypes, ancestry_counts, residuals, freqs):
    highest = lax.Precision.HIGHEST
    var_count = lax.axis_size("var")
    rows, width = genotypes.shape
    share = rows // var_count
    anc = freqs.shape[0]
    traits = residuals.shape[1]
    counts = ancestry_counts.astype(F32)
    fractions = counts / jnp.sum(counts, axis=1, keepdims=True)
    dosage = genotypes.astype(F32)
    recon = jnp.dot(fractions, freqs, precision=highest)
    ratio_a = dosage / recon
    ratio_b = (2.0 - dosage) / (1.0 - recon)
    excess = ratio_a - ratio_b
    gradient, second = lax.psum(
        (jnp.dot(excess, freqs.T, precision=highest), jnp.sum(ratio_b, axis=1)), "var"
    )
    excess_sum, second_sum = lax.psum(
        (
            jnp.dot(fractions.T, excess, precision=highest),
            jnp.dot(fractions.T, ratio_b, precision=highest),
        ),
        "smp",
    )
    freq_next, freq_gradient = update_freqs(
        freqs, excess_sum, second_sum, rows * lax.axis_size("smp")
    )
    weighted = fractions * (gradient + second[:, None])
    q_new = weighted / jnp.sum(weighted, axis=1, keepdims=True)
    first_row = lax.axis_index("var") * share
    own_next = lax.dynamic_slice_in_dim(q_new, first_row, share, 0)
    own_gradient = lax.dynamic_slice_in_dim(gradient, first_row, share, 0)
    ratio = dosage / jnp.dot(q_new, freqs, precision=highest)
    residual = residuals.astype(F32) / 1000.0
    products = (q_new[:, :, None] * residual[:, None, :]).reshape(rows, anc * traits)
    score, info = lax.psum(
        (
            jnp.dot(products.T, ratio, precision=highest),
            jnp.dot((q_new * q_new).T, ratio * ratio, precision=highest),
        ),
        "smp",
    )
    tiles = score.reshape(anc, traits, width)
    z_score = tiles / jnp.sqrt(info + 1e-06)[:, None, :]
    return (own_next, own_gradient / math.sqrt(width * var_count), freq_next, freq_gradient, z_score)


def solution(mesh):
    sizes = dict(mesh.shape)

    def step(genotypes, ancestry_counts, residuals, freqs):
        rows = genotypes.shape[0] // (sizes["grp"] * sizes["smp"])
        power = sizes["var"] & (sizes["var"] - 1) == 0 and sizes["var"] >= 4
        tiled = rows % (16 * sizes["var"]) == 0 and rows % (2 * LANES) == 0
        in_specs = (
            P(("grp", "smp"), "var"),
            P(("grp", "smp"), None),
            P(("grp", "smp"), None),
            P("grp", "var"),
        )
        out_specs = (
            P(("grp", "smp", "var"), None),
            P(("grp", "smp", "var"), None),
            P("grp", "var"),
            P("grp", "var"),
            P("grp", None, "var"),
        )
        fits = power and tiled and sizes["smp"] == 2

        def body(*args):
            return (shards if fits else plain_shards)(*args)

        mapped = jax.shard_map(
            body,
            mesh=mesh,
            in_specs=in_specs,
            out_specs=out_specs,
            check_vma=False,
        )
        return mapped(genotypes, ancestry_counts, residuals, freqs)

    return step
```
